32 devices in a mesh: dp: 8 (over z, y), tensor: 4 (over x, core).
Axes of the slice: x: 2, y: 2, z: 4, core: 2. Of those that a mesh axis runs over, the one named last changes fastest.
Arguments:
- tokens: bfloat16 [512, 1536], P('dp'), may hold values from -6 to 6
- norm_gain: float32 [1536], replicated, may hold values from 0.1 to 1.9
- w_query: bfloat16 [1536, 1024], P(None, 'tensor'), may hold values from -0.15625 to 0.15625
- w_keyval: bfloat16 [1536, 256], replicated, may hold values from -0.15625 to 0.15625
- w_out: bfloat16 [1024, 1536], P('tensor'), may hold values from -0.5 to 0.5
- kv_pool: bfloat16 [4096, 128, 256], P(('dp', 'tensor')), may hold values from -256 to 256
- page_table: int32 [512, 8], P('dp', 'tensor'), may hold values from 0 to 127, as said below
- positions: int32 [512], P('dp'), may hold values from 0 to 8191
- assignment: int32 [512], P('dp'), may hold values from 0 to 511, as said below
Outputs:
- attn_out: bfloat16 [512, 1536], P('dp')
The draws below stay inside these ranges and needn't reach their ends.
Inputs may be any that keep to these rules, and one draw needn't show every extreme that they name: `assignment`: the serving slot is the serving device's dp index times 64 plus a local slot; each serving slot is taken by exactly one request; the 64 requests of one device go to 8 distinct devices, exactly 8 to each. `page_table`: on each device the entries form a permutation of 0 to 127.
All inputs are finite; a program needn't handle non-finite values.
Results may differ from the reference program's by a relative error of at most 0.03.
Values may be sent and summed in bfloat16 or wider, within the bound.
A program may use at most 64 MiB of HBM per device.

```python
import math
import jax
import jax.numpy as jnp
from jax import lax

D = 1536
HEADS = 8
HD = 128
WINDOW = 1024
PAGE = 128
R_DEV = 64
CYCLE = 8
PPD = 2
POOL_DEV = 128
CAP = 8
REQ = 512
N_DP = 8
N_TENSOR = 4


def draw_kv_pool(key, part):
    first_key = jax.random.fold_in(key, 0)
    shape = (N_DP * N_TENSOR * POOL_DEV, PAGE, 2 * HD)
    base = jnp.clip(jax.random.normal(first_key, shape, jnp.float32), -4.0, 4.0)
    keys_part = base[..., :HD] * 2.0
    values_part = base[..., HD:]
    return jnp.concatenate([keys_part, values_part], axis=-1).astype(jnp.bfloat16)


def draw_page_table(key, part):
    subkeys = jax.random.split(key, N_DP * N_TENSOR)
    perms = jax.vmap(lambda k: jax.random.permutation(k, POOL_DEV))(subkeys)
    perms = perms.reshape(N_DP, N_TENSOR, R_DEV, PPD).transpose(0, 2, 1, 3)
    return perms.reshape(N_DP * R_DEV, N_TENSOR * PPD).astype(jnp.int32)


def draw_positions(key, part):
    first_key, second_key, third_key, fourth_key = jax.random.split(key, 4)
    highest = int(math.log2(WINDOW)) + 3
    powers = jax.random.randint(first_key, (REQ,), 3, highest + 1)
    limits = jnp.left_shift(jnp.ones((REQ,), jnp.int32), powers)
    drawn = jax.random.randint(second_key, (REQ,), 0, limits).astype(jnp.int32)
    top_index = jax.random.randint(third_key, (), 0, REQ)
    low_index = (top_index + 1 + jax.random.randint(fourth_key, (), 0, REQ - 1)) % REQ
    drawn = drawn.at[top_index].set(8 * WINDOW - 1)
    drawn = drawn.at[low_index].set(0)
    return drawn.astype(jnp.int32)


def draw_assignment(key, part):
    first_key, second_key, third_key = jax.random.split(key, 3)
    groups = R_DEV // CAP
    offsets = jax.random.permutation(first_key, N_DP)[:groups]
    ranks = jax.vmap(lambda k: jax.random.permutation(k, R_DEV))(jax.random.split(second_key, N_DP))
    sigma = jax.vmap(lambda k: jax.random.permutation(k, R_DEV))(jax.random.split(third_key, N_DP))
    homes = jnp.arange(N_DP)[:, None]
    group_of = ranks // CAP
    within = ranks % CAP
    target = (homes + offsets[group_of]) % N_DP
    local = sigma[target, group_of * CAP + within]
    return (target * R_DEV + local).reshape(-1).astype(jnp.int32)


def shard_levels(stream_key, shape, shards, smallest, high):
    factor_of = 1.0
    for position, parts in shards:
        heights = jax.random.uniform(jax.random.fold_in(jax.random.fold_in(stream_key, 6), position), (parts,), jnp.float32, smallest / len(shards), high / len(shards))
        factor_of = factor_of * jnp.repeat(jnp.exp(heights), shape[position] // parts).reshape((-1,) + (1,) * (len(shape) - 1 - position))
    return factor_of


def centred(stream_key, dims, scale, reach, cuts=(), held_as=jnp.bfloat16):
    factor_of = shard_levels(stream_key, dims, cuts, -0.22, 0.18) if cuts else 1.0
    values = jax.random.normal(stream_key, dims, jnp.float32) * scale * factor_of
    return jnp.minimum(jnp.maximum(values, -reach), reach).astype(held_as)


def setup_inputs(seed: int = 0) -> dict:
    keys = jax.random.split(jax.random.key(seed), 10)
    tokens = centred(keys[0], (REQ, D), 1.0, 6.0, ((0, 8),))
    norm_gain = jnp.clip(1.0 + 0.18 * jax.random.normal(keys[1], (D,), jnp.float32), 0.1, 1.9)
    w_query = centred(keys[2], (D, HEADS * HD), D ** -0.5, 0.15625, ((1, 4),))
    w_keyval = centred(keys[3], (D, 2 * HD), D ** -0.5, 0.15625)
    w_out = centred(keys[4], (HEADS * HD, D), HD ** -0.5, 0.5, ((0, 4),))
    kv_pool = draw_kv_pool(jax.random.fold_in(keys[9], 71), 0)
    page_table = draw_page_table(jax.random.fold_in(keys[9], 71), 0)
    positions = draw_positions(jax.random.fold_in(keys[9], 71), 0)
    assignment = draw_assignment(jax.random.fold_in(keys[9], 71), 0)
    return dict(tokens=tokens, norm_gain=norm_gain, w_query=w_query, w_keyval=w_keyval, w_out=w_out, kv_pool=kv_pool, page_table=page_table, positions=positions, assignment=assignment)


def rotate(values, where, width):
    half = width // 2
    freqs = 10000.0 ** (-jnp.arange(half, dtype=jnp.float32) * 2.0 / width)
    angles = where.astype(jnp.float32)[..., None] * freqs
    cosine = jnp.cos(angles)
    sine = jnp.sin(angles)
    first = values[..., :half]
    second = values[..., half:]
    return jnp.concatenate([first * cosine - second * sine, first * sine + second * cosine], axis=-1)

def reference(tokens, norm_gain, w_query, w_keyval, w_out, kv_pool, page_table, positions, assignment):
    floats = tokens.astype(jnp.float32)
    normed = (floats * lax.rsqrt(lax.optimization_barrier(jnp.mean(floats * floats, axis=-1, keepdims=True)) + 1e-06) * norm_gain).astype(jnp.bfloat16)
    query = jnp.dot(normed, w_query, preferred_element_type=jnp.float32).reshape(REQ, HEADS, HD)
    query = rotate(query, positions[:, None], HD).astype(jnp.bfloat16)
    key_value = jnp.dot(normed, w_keyval, preferred_element_type=jnp.float32)
    new_key = rotate(key_value[:, :HD], positions, HD).astype(jnp.bfloat16)
    new_value = key_value[:, HD:].astype(jnp.bfloat16)
    serve_dev = (assignment // R_DEV).astype(jnp.int32)
    table = page_table[assignment]
    owner = (jnp.arange(CYCLE) // PPD).astype(jnp.int32)
    global_page = ((serve_dev[:, None] * N_TENSOR + owner[None, :]) * POOL_DEV + table).astype(jnp.int32)
    scale = HD ** (-0.5)

    def block(pieces):
        q_block, k_block, v_block, p_block, g_block = pieces
        page_entries = kv_pool[g_block].reshape(R_DEV, WINDOW, 2 * HD).astype(jnp.float32)
        q_float = q_block.astype(jnp.float32)
        scores = jnp.einsum('rhd,rkd->rhk', q_float, page_entries[..., :HD]) * scale
        own = jnp.einsum('rhd,rd->rh', q_float, k_block.astype(jnp.float32)) * scale
        offset = jnp.mod(jnp.arange(WINDOW, dtype=jnp.int32)[None, :] - p_block[:, None], WINDOW)
        valid = (offset != 0) & (p_block[:, None] - WINDOW + offset >= 0)
        scores = jnp.where(valid[:, None, :], scores, -jnp.inf)
        top = jnp.maximum(lax.optimization_barrier(jnp.max(scores, axis=2)), own)
        weight_tensors = jnp.exp(scores - top[..., None])
        own_weight = jnp.exp(own - top)
        total = lax.optimization_barrier(jnp.sum(weight_tensors, axis=2)) + own_weight
        weights_low = lax.optimization_barrier(weight_tensors.astype(jnp.bfloat16)).astype(jnp.float32)
        local_lower_index = lax.optimization_barrier(own_weight.astype(jnp.bfloat16)).astype(jnp.float32)
        summed = jnp.einsum('rhk,rkd->rhd', weights_low, page_entries[..., HD:])
        summed = summed + local_lower_index[..., None] * v_block.astype(jnp.float32)[:, None, :]
        return (summed / total[..., None]).astype(jnp.bfloat16)
    attended = lax.map(block, (query.reshape(N_DP, R_DEV, HEADS, HD), new_key.reshape(N_DP, R_DEV, HD), new_value.reshape(N_DP, R_DEV, HD), positions.reshape(N_DP, R_DEV), global_page.reshape(N_DP, R_DEV, CYCLE)))
    attended = attended.reshape(REQ, HEADS * HD)
    return jnp.dot(attended, w_out, preferred_element_type=jnp.float32).astype(jnp.bfloat16)
```

```python
import functools
import math

import jax
import jax.numpy as jnp
from jax import lax
from jax.experimental import pallas as pl
from jax.experimental.pallas import tpu as pltpu
from jax.sharding import PartitionSpec as P

masked_score = -1e30
peak_floor = -1e29
norm_eps = 1e-06
rotary_base = 10000.0
chunks = 8
MESH = pl.DeviceIdType.MESH
f32 = jnp.float32
bf16 = jnp.bfloat16


def dot(a, b):
    return jnp.dot(a, b, preferred_element_type=f32)


def dot_t(a, b):
    return lax.dot_general(a, b, (((1,), (1,)), ((), ())), preferred_element_type=f32)


def iota(shape, axis):
    return lax.broadcasted_iota(jnp.int32, shape, axis)


def xor(a, b, n):
    out, bit = 0, 1
    while bit < n:
        out = out + bit * lax.rem(lax.div(a, bit) + lax.div(b, bit), 2)
        bit *= 2
    return out


def kernel(
    n_dp,
    n_tensor,
    capacity,
    tokens_hbm,
    gain_hbm,
    wq_hbm,
    wkv_hbm,
    wo_hbm,
    pool_hbm,
    table_hbm,
    position_hbm,
    assign_hbm,
    out_ref,
    tokens,
    gain_ref,
    table_ref,
    position_ref,
    assign_ref,
    wq,
    wkv,
    wo,
    pool,
    q_out,
    meta_out,
    q_in,
    meta_in,
    meta_s,
    group_q,
    group_acc,
    stat_out,
    stat_in,
    small_out,
    small_in,
    sum_out,
    sum_in,
    pair_sum,
    load_sem,
    pool_sem,
    send_sem,
    recv_sem,
    meta_sem,
    smem_sem,
    q_sem,
    stat_sem,
    small_sem,
):
    dp = lax.axis_index("dp")
    tp = lax.axis_index("tensor")
    n_all = n_dp * n_tensor
    me = tp * n_dp + dp
    rows = tokens.shape[0]
    slots = n_dp * capacity
    width = wkv.shape[1] // 2
    half = width // 2
    local_heads = wq.shape[1] // width
    heads = local_heads * n_tensor
    pages, page_len = pool.shape[0], pool.shape[1]
    page_rows = table_ref.shape[0]
    window = page_rows * n_tensor * page_len
    chunk = pages // chunks
    scale = width ** (-0.5)
    out_rows = rows // n_tensor

    barrier = pltpu.get_barrier_semaphore()

    def peer_of(i):
        other = lax.rem(me + i, n_all)
        return lax.rem(other, n_dp), lax.div(other, n_dp)

    @pl.loop(1, n_all)
    def _(i):
        pl.semaphore_signal(barrier, inc=1, device_id=peer_of(i), device_id_type=MESH)

    loads = [
        pltpu.make_async_copy(src, dst, load_sem.at[i])
        for i, (src, dst) in enumerate(
            (
                (position_hbm, position_ref),
                (assign_hbm, assign_ref),
                (tokens_hbm, tokens),
                (gain_hbm, gain_ref),
                (wq_hbm, wq),
                (table_hbm, table_ref),
                (wkv_hbm, wkv),
                (wo_hbm, wo),
            )
        )
    ]
    for load in loads:
        load.start()

    def pool_load(i):
        part = pl.ds(i * chunk, chunk)
        return pltpu.make_async_copy(pool_hbm.at[part], pool.at[part], pool_sem.at[i])

    for i in range(chunks):
        pool_load(i).start()

    eye = iota((rows, rows), 0) == iota((rows, rows), 1)
    before = iota((rows, rows), 1) < iota((rows, rows), 0)
    after = iota((rows, rows), 1) > iota((rows, rows), 0)

    def as_column(row):
        return jnp.sum(jnp.where(eye, row, 0.0), axis=1, keepdims=True)

    loads[0].wait()
    loads[1].wait()
    position_row = position_ref[...].astype(f32)
    position = as_column(position_row)
    target_int = lax.div(assign_ref[...], rows)
    slot_row = (assign_ref[...] - target_int * rows).astype(f32)
    target_row = target_int.astype(f32)
    target = as_column(target_row)
    slot = as_column(slot_row)
    same = (target == target_row).astype(f32)
    place_row = target_row * capacity + jnp.sum(
        jnp.where(after, same, 0.0), axis=0, keepdims=True
    )
    within = jnp.sum(jnp.where(before, same, 0.0), axis=1, keepdims=True)
    place = target * capacity + within
    routed = (iota((slots, rows), 0).astype(f32) == place_row).astype(bf16)
    from_place = iota((rows, slots), 1).astype(f32) == place
    high = jnp.floor(position * (1.0 / 128.0))
    low = position - high * 128.0
    lane = iota((rows, 128), 1).astype(f32)
    fields = jnp.where(
        lane == within,
        slot,
        jnp.where(
            lane == within + capacity,
            high,
            jnp.where(lane == within + 2 * capacity, low, 0.0),
        ),
    ).astype(bf16)
    to_device = (iota((n_dp, rows), 0).astype(f32) == target_row).astype(bf16)
    meta = dot(to_device, fields).astype(jnp.int32)
    for d in range(n_dp):
        meta_out[d] = meta[d : d + 1, :]

    step = -2.0 * math.log(rotary_base) / width
    angles = position * jnp.exp(iota((1, half), 1).astype(f32) * step)
    cosine = jnp.cos(angles)
    sine = jnp.sin(angles)

    def rotate(values):
        first, second = values[:, :half], values[:, half:]
        return jnp.concatenate(
            [first * cosine - second * sine, first * sine + second * cosine], axis=1
        )

    loads[2].wait()
    loads[3].wait()
    gain = jnp.concatenate([gain_ref[i : i + 1, :] for i in range(gain_ref.shape[0])], axis=1)
    floats = tokens[...].astype(f32)
    normed = (
        floats
        * lax.rsqrt(jnp.mean(floats * floats, axis=-1, keepdims=True) + norm_eps)
        * gain
    ).astype(bf16)
    loads[4].wait()
    raw = dot(normed, wq[...])
    query = jnp.concatenate(
        [rotate(raw[:, h * width : (h + 1) * width]) for h in range(local_heads)], axis=1
    ).astype(bf16)
    q_out[...] = dot(routed, query).reshape(n_dp, capacity, local_heads * width).astype(bf16)

    pl.semaphore_wait(barrier, n_all - 1)

    def remote(src, dst, sent, received, where):
        return pltpu.make_async_remote_copy(
            src_ref=src,
            dst_ref=dst,
            send_sem=sent,
            recv_sem=received,
            device_id=where,
            device_id_type=MESH,
        )

    def wait_for(ref, sem):
        pltpu.make_async_copy(ref, ref, sem).wait()

    @pl.loop(1, n_dp)
    def _(i):
        d = xor(dp, i, n_dp)
        remote(meta_out.at[d], meta_in.at[dp], send_sem.at[0], meta_sem.at[dp], (d, tp)).start()

    pltpu.make_async_copy(meta_out.at[dp], meta_in.at[dp], meta_sem.at[dp]).start()

    @pl.loop(1, n_all)
    def _(i):
        d = xor(dp, lax.div(i, n_tensor), n_dp)
        t = xor(tp, lax.rem(i, n_tensor), n_tensor)
        remote(q_out.at[d], q_in.at[dp, tp], send_sem.at[1], q_sem.at[dp], (d, t)).start()

    pltpu.make_async_copy(q_out.at[dp], q_in.at[dp, tp], q_sem.at[dp]).start()

    loads[6].wait()
    key_value = dot(normed, wkv[...])
    new_key = rotate(key_value[:, :width]).astype(bf16).astype(f32)
    new_value = key_value[:, width:].astype(bf16).astype(f32)
    own_scores = []
    for h in range(local_heads):
        product = query[:, h * width : (h + 1) * width].astype(f32) * new_key
        column = jnp.sum(product, axis=1, keepdims=True) * scale
        own_scores.append(jnp.sum(jnp.where(from_place, column, 0.0), axis=0, keepdims=True))
    own_score = jnp.concatenate(own_scores, axis=0)

    loads[5].wait()
    for i in range(chunks):
        pool_load(i).wait()

    lane_key = tp * page_rows * page_len + iota((heads, page_len), 1)
    stat_lane = iota((heads, 2 * slots), 1)

    def fetch(g):
        return pltpu.make_async_copy(meta_in.at[g], meta_s.at[g], smem_sem.at[g])

    def start_fetch(g):
        wait_for(meta_in.at[g], meta_sem.at[g])
        fetch(g).start()

    start_fetch(dp)

    @pl.loop(0, n_dp)
    def _(i):
        g = xor(dp, i, n_dp)
        fetch(g).wait()

        @pl.when(i + 1 < n_dp)
        def _():
            start_fetch(xor(dp, i + 1, n_dp))

        wait_for(q_in.at[g], q_sem.at[g])
        for t in range(n_tensor):
            part = q_in[g, t].astype(f32)
            for h in range(local_heads):
                group_q[pl.ds(t * local_heads + h, capacity, stride=heads), :] = part[
                    :, h * width : (h + 1) * width
                ]
        ids, scored = [], []
        for r in range(capacity):
            at = jnp.clip(meta_s[g, 0, r], 0, rows - 1)
            where = meta_s[g, 0, capacity + r] * 128 + meta_s[g, 0, 2 * capacity + r]
            ids.append([table_ref[j, at] for j in range(page_rows)])
            q = group_q[r * heads : (r + 1) * heads, :].astype(bf16)
            parts = []
            for j in range(page_rows):
                offset = (lane_key + (j * page_len) - where) & (window - 1)
                live = (offset != 0) & (offset >= window - where)
                keys = pool[ids[r][j], :, :width]
                parts.append(jnp.where(live, dot_t(q, keys) * scale, masked_score))
            scored.append(jnp.concatenate(parts, axis=1))
        packed = jnp.zeros((heads, 2 * slots), f32)
        for r in range(capacity):
            top = jnp.maximum(jnp.max(scored[r], axis=1, keepdims=True), peak_floor)
            weight = jnp.exp(scored[r] - top)
            total = jnp.sum(weight, axis=1, keepdims=True)
            values = jnp.concatenate(
                [pool[ids[r][j], :, width:] for j in range(page_rows)], axis=0
            )
            group_acc[r * heads : (r + 1) * heads, :] = dot(weight.astype(bf16), values)
            spot = dp * capacity + r
            packed = jnp.where(stat_lane == spot, top, packed)
            packed = jnp.where(stat_lane == spot + slots, total, packed)
        for t in range(n_tensor):
            small_out[g, t] = packed[t * local_heads : (t + 1) * local_heads, :]
            stat_out[g, t] = jnp.concatenate(
                [
                    group_acc[pl.ds(t * local_heads + h, capacity, stride=heads), :]
                    for h in range(local_heads)
                ],
                axis=1,
            ).astype(bf16)

        @pl.loop(0, n_tensor)
        def _(k):
            t = xor(tp, n_tensor - 1 - k, n_tensor)
            here = (i == 0) & (k == n_tensor - 1)

            @pl.when(jnp.logical_not(here))
            def _():
                remote(
                    small_out.at[g, t], small_in.at[tp, dp], send_sem.at[5], small_sem.at[dp], (g, t)
                ).start()
                remote(
                    stat_out.at[g, t], stat_in.at[tp, dp], send_sem.at[2], stat_sem.at[dp], (g, t)
                ).start()

            @pl.when(here)
            def _():
                pltpu.make_async_copy(
                    small_out.at[g, t], small_in.at[tp, dp], small_sem.at[dp]
                ).start()
                pltpu.make_async_copy(
                    stat_out.at[g, t], stat_in.at[tp, dp], stat_sem.at[dp]
                ).start()

    loads[7].wait()

    @pl.loop(0, n_dp)
    def _(i):
        g = xor(dp, i, n_dp)
        wait_for(small_in.at[0, pl.ds(0, n_tensor)], small_sem.at[g])
        wait_for(stat_in.at[0, pl.ds(0, n_tensor)], stat_sem.at[g])

    tops, sums = [], []
    for t in range(n_tensor):
        merged = jnp.sum(small_in[t], axis=0)
        tops.append(merged[:, :slots])
        sums.append(merged[:, slots:])
    overall = functools.reduce(jnp.maximum, tops, own_score)
    fresh = jnp.exp(own_score - overall)
    keeps = [jnp.exp(top - overall) for top in tops]
    total = functools.reduce(jnp.add, [k * s for k, s in zip(keeps, sums)], fresh)
    attended = []
    for h in range(local_heads):
        row = slice(h, h + 1)
        acc = (
            jnp.sum(jnp.where(from_place, fresh[row] / total[row], 0.0), axis=1, keepdims=True)
            * new_value
        )
        for t in range(n_tensor):
            factor = jnp.where(from_place, keeps[t][row] / total[row], 0.0).astype(bf16)
            part = stat_in[t, :, :, h * width : (h + 1) * width].astype(f32)
            acc = acc + dot(factor, part.reshape(slots, width).astype(bf16))
        attended.append(acc)
    attended = jnp.concatenate(attended, axis=1).astype(bf16)
    partial = dot(attended, wo[...])
    sum_out[...] = partial.reshape(n_tensor, out_rows, partial.shape[1]).astype(bf16)

    parity = lax.rem(tp, 2)
    sibling = tp + 1 - 2 * parity
    opposite = lax.rem(tp + 2, n_tensor)
    mine = pl.ds(2 * parity, 2)
    theirs = pl.ds(2 - 2 * parity, 2)
    remote(
        sum_out.at[theirs], sum_in.at[0:2], send_sem.at[3], recv_sem.at[0], (dp, sibling)
    ).start()
    wait_for(sum_in.at[0:2], recv_sem.at[0])
    pair_sum[...] = (sum_out[mine].astype(f32) + sum_in[0:2].astype(f32)).astype(bf16)
    remote(pair_sum, sum_in.at[2:4], send_sem.at[4], recv_sem.at[1], (dp, opposite)).start()
    wait_for(sum_in.at[2:4], recv_sem.at[1])
    out_ref[mine] = (pair_sum[...].astype(f32) + sum_in[2:4].astype(f32)).astype(bf16)
    remote(
        out_ref.at[mine], out_ref.at[mine], send_sem.at[6], recv_sem.at[2], (dp, sibling)
    ).start()
    wait_for(out_ref.at[theirs], recv_sem.at[2])
    wait_for(meta_in.at[pl.ds(0, n_dp - 1)], send_sem.at[0])
    for _ in range(n_tensor - 1):
        wait_for(q_in.at[:, 0], send_sem.at[1])
        wait_for(stat_in.at[0], send_sem.at[2])
        wait_for(small_in.at[0], send_sem.at[5])
    wait_for(q_in.at[pl.ds(0, n_dp - 1), 0], send_sem.at[1])
    wait_for(stat_in.at[0, pl.ds(0, n_dp - 1)], send_sem.at[2])
    wait_for(small_in.at[0, pl.ds(0, n_dp - 1)], send_sem.at[5])
    for k in (3, 4, 6):
        wait_for(pair_sum, send_sem.at[k])


def local(tokens, norm_gain, w_query, w_keyval, w_out, kv_pool, page_table, positions, assignment):
    n_dp, n_tensor = lax.axis_size("dp"), lax.axis_size("tensor")
    rows, model = tokens.shape
    width = w_keyval.shape[1] // 2
    query_width = w_query.shape[1]
    local_heads = query_width // width
    heads = local_heads * n_tensor
    capacity = max(8, rows // n_dp)
    slots = n_dp * capacity
    whole = pl.BlockSpec(memory_space=pltpu.VMEM)
    far = pl.BlockSpec(memory_space=pltpu.HBM)
    out = pl.pallas_call(
        functools.partial(kernel, n_dp, n_tensor, capacity),
        out_shape=jax.ShapeDtypeStruct((n_tensor, rows // n_tensor, model), bf16),
        in_specs=[far] * 9,
        out_specs=whole,
        scratch_shapes=[
            pltpu.VMEM(tokens.shape, bf16),
            pltpu.VMEM((model // 128, 128), f32),
            pltpu.SMEM(page_table.shape[::-1], jnp.int32),
            pltpu.VMEM((1, rows), jnp.int32),
            pltpu.VMEM((1, rows), jnp.int32),
            pltpu.VMEM(w_query.shape, bf16),
            pltpu.VMEM(w_keyval.shape, bf16),
            pltpu.VMEM(w_out.shape, bf16),
            pltpu.VMEM(kv_pool.shape, bf16),
            pltpu.VMEM((n_dp, capacity, query_width), bf16),
            pltpu.VMEM((n_dp, 1, 128), jnp.int32),
            pltpu.VMEM((n_dp, n_tensor, capacity, query_width), bf16),
            pltpu.VMEM((n_dp, 1, 128), jnp.int32),
            pltpu.SMEM((n_dp, 1, 128), jnp.int32),
            pltpu.VMEM((capacity * heads, width), f32),
            pltpu.VMEM((capacity * heads, width), f32),
            pltpu.VMEM((n_dp, n_tensor, capacity, query_width), bf16),
            pltpu.VMEM((n_tensor, n_dp, capacity, query_width), bf16),
            pltpu.VMEM((n_dp, n_tensor, local_heads, 2 * slots), f32),
            pltpu.VMEM((n_tensor, n_dp, local_heads, 2 * slots), f32),
            pltpu.VMEM((n_tensor, rows // n_tensor, model), bf16),
            pltpu.VMEM((n_tensor, rows // n_tensor, model), bf16),
            pltpu.VMEM((2, rows // n_tensor, model), bf16),
            pltpu.SemaphoreType.DMA((8,)),
            pltpu.SemaphoreType.DMA((chunks,)),
            pltpu.SemaphoreType.DMA((7,)),
            pltpu.SemaphoreType.DMA((3,)),
            pltpu.SemaphoreType.DMA((n_dp,)),
            pltpu.SemaphoreType.DMA((n_dp,)),
            pltpu.SemaphoreType.DMA((n_dp,)),
            pltpu.SemaphoreType.DMA((n_dp,)),
            pltpu.SemaphoreType.DMA((n_dp,)),
        ],
        compiler_params=pltpu.CompilerParams(
            collective_id=0, has_side_effects=True, vmem_limit_bytes=62 << 20
        ),
    )(
        tokens,
        norm_gain.reshape(model // 128, 128),
        w_query,
        w_keyval,
        w_out,
        kv_pool,
        page_table.T,
        positions.reshape(1, rows),
        assignment.reshape(1, rows),
    )
    return out.reshape(rows, model)


def solution(mesh):
    return jax.shard_map(
        local,
        mesh=mesh,
        in_specs=(
            P("dp", None),
            P(),
            P(None, "tensor"),
            P(),
            P("tensor", None),
            P(("dp", "tensor"), None, None),
            P("dp", "tensor"),
            P("dp"),
            P("dp"),
        ),
        out_specs=P("dp", None),
        check_vma=False,
    )
```

```python
import functools
import math

import jax
import jax.numpy as jnp
from jax import lax
from jax.experimental import pallas as pl
from jax.experimental.pallas import tpu as pltpu
from jax.sharding import PartitionSpec as P

masked_score = -1e30
peak_floor = -1e29
norm_eps = 1e-06
rotary_base = 10000.0
chunks = 8
MESH = pl.DeviceIdType.MESH
f32 = jnp.float32
bf16 = jnp.bfloat16


def dot(a, b):
    return jnp.dot(a, b, preferred_element_type=f32)


def dot_t(a, b):
    return lax.dot_general(a, b, (((1,), (1,)), ((), ())), preferred_element_type=f32)


def iota(shape, axis):
    return lax.broadcasted_iota(jnp.int32, shape, axis)


def xor(a, b, n):
    out, bit = 0, 1
    while bit < n:
        out = out + bit * lax.rem(lax.div(a, bit) + lax.div(b, bit), 2)
        bit *= 2
    return out


def turn(i, n):
    return jnp.where(i < n // 2, i, n - 1 - i + n // 2)


def kernel(
    n_dp,
    n_tensor,
    capacity,
    tokens_hbm,
    gain_hbm,
    wq_hbm,
    wkv_hbm,
    wo_hbm,
    pool_hbm,
    table_hbm,
    position_hbm,
    assign_hbm,
    out_ref,
    tokens,
    gain_ref,
    table_ref,
    position_ref,
    assign_ref,
    wq,
    wkv,
    wo,
    pool,
    q_out,
    meta_out,
    q_in,
    meta_in,
    meta_s,
    group_q,
    group_acc,
    stat_out,
    stat_in,
    small_out,
    small_in,
    part_out,
    part_in,
    sums,
    load_sem,
    pool_sem,
    send_sem,
    sum_sem,
    meta_sem,
    smem_sem,
    q_sem,
    stat_sem,
    small_sem,
):
    dp = lax.axis_index("dp")
    tp = lax.axis_index("tensor")
    n_all = n_dp * n_tensor
    me = tp * n_dp + dp
    rows = tokens.shape[0]
    slots = n_dp * capacity
    width = wkv.shape[1] // 2
    half = width // 2
    local_heads = wq.shape[1] // width
    heads = local_heads * n_tensor
    pages, page_len = pool.shape[0], pool.shape[1]
    page_rows = table_ref.shape[0]
    window = page_rows * n_tensor * page_len
    chunk = pages // chunks
    scale = width ** (-0.5)
    late = max(1, n_dp // 2)
    spans = ((0, n_dp - late), (n_dp - late, n_dp))

    def partner(i):
        return xor(dp, turn(i, n_dp), n_dp)

    barrier = pltpu.get_barrier_semaphore()

    def peer_of(i):
        other = lax.rem(me + i, n_all)
        return lax.rem(other, n_dp), lax.div(other, n_dp)

    loads = [
        pltpu.make_async_copy(src, dst, load_sem.at[i])
        for i, (src, dst) in enumerate(
            (
                (position_hbm, position_ref),
                (assign_hbm, assign_ref),
                (tokens_hbm, tokens),
                (gain_hbm, gain_ref),
                (wq_hbm, wq),
                (table_hbm, table_ref),
                (wkv_hbm, wkv),
                (wo_hbm, wo),
            )
        )
    ]
    for load in loads[:5]:
        load.start()

    @pl.loop(1, n_all)
    def _(i):
        pl.semaphore_signal(barrier, inc=1, device_id=peer_of(i), device_id_type=MESH)

    def pool_load(i):
        part = pl.ds(i * chunk, chunk)
        return pltpu.make_async_copy(pool_hbm.at[part], pool.at[part], pool_sem.at[i])


    for load in loads[5:]:
        load.start()
    for i in range(chunks):
        pool_load(i).start()

    eye = iota((rows, rows), 0) == iota((rows, rows), 1)
    before = iota((rows, rows), 1) < iota((rows, rows), 0)
    after = iota((rows, rows), 1) > iota((rows, rows), 0)

    def as_column(row):
        return jnp.sum(jnp.where(eye, row, 0.0), axis=1, keepdims=True)

    loads[0].wait()
    loads[1].wait()
    position_row = position_ref[...].astype(f32)
    position = as_column(position_row)
    target_int = lax.div(assign_ref[...], rows)
    slot_row = (assign_ref[...] - target_int * rows).astype(f32)
    target_row = turn(target_int ^ dp, n_dp).astype(f32)
    target = as_column(target_row)
    slot = as_column(slot_row)
    same = (target == target_row).astype(f32)
    place_row = target_row * capacity + jnp.sum(
        jnp.where(after, same, 0.0), axis=0, keepdims=True
    )
    within = jnp.sum(jnp.where(before, same, 0.0), axis=1, keepdims=True)
    place = target * capacity + within
    routed = (iota((slots, rows), 0).astype(f32) == place_row).astype(bf16)
    from_place = iota((rows, slots), 1).astype(f32) == place
    high = jnp.floor(position * (1.0 / 128.0))
    low = position - high * 128.0
    lane = iota((rows, 128), 1).astype(f32)
    fields = jnp.where(
        lane == within,
        slot,
        jnp.where(
            lane == within + capacity,
            high,
            jnp.where(lane == within + 2 * capacity, low, 0.0),
        ),
    ).astype(bf16)
    to_device = (iota((n_dp, rows), 0).astype(f32) == target_row).astype(bf16)
    meta = dot(to_device, fields).astype(jnp.int32)
    for d in range(n_dp):
        meta_out[d] = meta[d : d + 1, :]

    step = -2.0 * math.log(rotary_base) / width
    angles = position * jnp.exp(iota((1, half), 1).astype(f32) * step)
    cosine = jnp.cos(angles)
    sine = jnp.sin(angles)

    def rotate(values):
        first, second = values[:, :half], values[:, half:]
        return jnp.concatenate(
            [first * cosine - second * sine, first * sine + second * cosine], axis=1
        )

    loads[2].wait()
    loads[3].wait()
    gain = jnp.concatenate([gain_ref[i : i + 1, :] for i in range(gain_ref.shape[0])], axis=1)
    floats = tokens[...].astype(f32)
    normed = (
        floats
        * lax.rsqrt(jnp.mean(floats * floats, axis=-1, keepdims=True) + norm_eps)
        * gain
    ).astype(bf16)
    loads[4].wait()
    raw = dot(normed, wq[...])
    query = jnp.concatenate(
        [rotate(raw[:, h * width : (h + 1) * width]) for h in range(local_heads)], axis=1
    ).astype(bf16)
    q_out[...] = dot(routed, query).reshape(n_dp, capacity, local_heads * width).astype(bf16)

    pl.semaphore_wait(barrier, n_all - 1)

    def remote(src, dst, sent, received, where):
        return pltpu.make_async_remote_copy(
            src_ref=src,
            dst_ref=dst,
            send_sem=sent,
            recv_sem=received,
            device_id=where,
            device_id_type=MESH,
        )

    def wait_for(ref, sem):
        pltpu.make_async_copy(ref, ref, sem).wait()

    pltpu.make_async_copy(meta_out.at[0], meta_in.at[0], meta_sem.at[0]).start()

    @pl.loop(1, n_dp)
    def _(i):
        where = (partner(i), tp)
        remote(meta_out.at[i], meta_in.at[i], send_sem.at[0], meta_sem.at[i], where).start()

    pltpu.make_async_copy(q_out.at[0], q_in.at[0, tp], q_sem.at[0]).start()
    for k in range(1, n_tensor):
        where = (dp, xor(tp, k, n_tensor))
        remote(q_out.at[0], q_in.at[0, tp], send_sem.at[1], q_sem.at[0], where).start()

    @pl.loop(1, n_dp)
    def _(s):
        i = jnp.where(s <= n_dp // 2, n_dp // 2 + s - 1, s - n_dp // 2)
        d = partner(i)
        for k in reversed(range(n_tensor)):
            where = (d, xor(tp, k, n_tensor))
            remote(q_out.at[i], q_in.at[i, tp], send_sem.at[1], q_sem.at[i], where).start()

    loads[6].wait()
    key_value = dot(normed, wkv[...])
    new_key = rotate(key_value[:, :width]).astype(bf16).astype(f32)
    new_value = key_value[:, width:].astype(bf16).astype(f32)
    own_scores = []
    for h in range(local_heads):
        product = query[:, h * width : (h + 1) * width].astype(f32) * new_key
        column = jnp.sum(product, axis=1, keepdims=True) * scale
        own_scores.append(jnp.sum(jnp.where(from_place, column, 0.0), axis=0, keepdims=True))
    own_score = jnp.concatenate(own_scores, axis=0)
    placed_value = dot(routed, new_value.astype(bf16))

    loads[5].wait()
    for i in range(chunks):
        pool_load(i).wait()

    lane_key = tp * page_rows * page_len + iota((heads, page_len), 1)
    stat_lane = iota((heads, 2 * slots), 1)

    def fetch(g):
        return pltpu.make_async_copy(meta_in.at[g], meta_s.at[g], smem_sem.at[g])

    def start_fetch(g):
        wait_for(meta_in.at[g], meta_sem.at[g])
        fetch(g).start()

    start_fetch(0)

    @pl.loop(0, n_dp)
    def _(g):
        d = partner(g)
        fetch(g).wait()

        @pl.when(g + 1 < n_dp)
        def _():
            start_fetch(g + 1)

        wait_for(q_in.at[g], q_sem.at[g])
        for t in range(n_tensor):
            part = q_in[g, t].astype(f32)
            for h in range(local_heads):
                group_q[pl.ds(t * local_heads + h, capacity, stride=heads), :] = part[
                    :, h * width : (h + 1) * width
                ]
        ids, scored = [], []
        for r in range(capacity):
            at = jnp.clip(meta_s[g, 0, r], 0, rows - 1)
            where = meta_s[g, 0, capacity + r] * 128 + meta_s[g, 0, 2 * capacity + r]
            ids.append([table_ref[j, at] for j in range(page_rows)])
            q = group_q[r * heads : (r + 1) * heads, :].astype(bf16)
            parts = []
            for j in range(page_rows):
                offset = (lane_key + (j * page_len) - where) & (window - 1)
                live = (offset != 0) & (offset >= window - where)
                keys = pool[ids[r][j], :, :width]
                parts.append(jnp.where(live, dot_t(q, keys) * scale, masked_score))
            scored.append(jnp.concatenate(parts, axis=1))
        packed = jnp.zeros((heads, 2 * slots), f32)
        for r in range(capacity):
            top = jnp.maximum(jnp.max(scored[r], axis=1, keepdims=True), peak_floor)
            weight = jnp.exp(scored[r] - top)
            total = jnp.sum(weight, axis=1, keepdims=True)
            values = jnp.concatenate(
                [pool[ids[r][j], :, width:] for j in range(page_rows)], axis=0
            )
            group_acc[r * heads : (r + 1) * heads, :] = dot(weight.astype(bf16), values)
            spot = g * capacity + r
            packed = jnp.where(stat_lane == spot, top, packed)
            packed = jnp.where(stat_lane == spot + slots, total, packed)
        for t in range(n_tensor):
            small_out[g, t] = packed[t * local_heads : (t + 1) * local_heads, :]
            stat_out[g, t] = jnp.concatenate(
                [
                    group_acc[pl.ds(t * local_heads + h, capacity, stride=heads), :]
                    for h in range(local_heads)
                ],
                axis=1,
            ).astype(bf16)

        for k in reversed(range(n_tensor)):
            t = xor(tp, k, n_tensor)
            pairs = (
                (small_out.at[g, t], small_in.at[tp, g], send_sem.at[3], small_sem.at[g]),
                (stat_out.at[g, t], stat_in.at[tp, g], send_sem.at[2], stat_sem.at[g]),
            )

            def send():
                for src, dst, sent, received in pairs:
                    remote(src, dst, sent, received, (d, t)).start()

            if k:
                send()
            else:
                pl.when(g > 0)(send)

                @pl.when(g == 0)
                def _():
                    for src, dst, sent, received in pairs:
                        pltpu.make_async_copy(src, dst, received).start()

    loads[7].wait()
    sibling = (dp, xor(tp, 1, n_tensor))
    opposite = (dp, xor(tp, 2, n_tensor))

    def rows_of(part):
        low, high = spans[part]
        return low * capacity, (high - low) * capacity

    def to_sibling(part):
        low, count = rows_of(part)
        at = pl.ds(low, count)
        return remote(
            part_out.at[at], part_in.at[at], sum_sem.at[part], sum_sem.at[2 + part], sibling
        )

    def to_opposite(part):
        low, count = rows_of(part)
        own, other = pl.ds(2 * low, count), pl.ds(2 * low + count, count)
        return remote(
            sums.at[own], sums.at[other], sum_sem.at[4 + part], sum_sem.at[6 + part], opposite
        )

    def merge(part):
        first, last = spans[part]
        low, count = rows_of(part)

        @pl.loop(first, last)
        def _(g):
            wait_for(small_in.at[0, pl.ds(0, n_tensor)], small_sem.at[g])
            wait_for(stat_in.at[0, pl.ds(0, n_tensor)], stat_sem.at[g])

        tops, totals = [], []
        for t in range(n_tensor):
            merged = jnp.sum(small_in[t, first:last], axis=0)
            tops.append(merged[:, :slots])
            totals.append(merged[:, slots:])
        overall = functools.reduce(jnp.maximum, tops, own_score)
        fresh = jnp.exp(own_score - overall)
        keeps = [jnp.exp(top - overall) for top in tops]
        total = functools.reduce(jnp.add, [k * s for k, s in zip(keeps, totals)], fresh)
        spot = iota((count, slots), 1) == iota((count, slots), 0) + low

        def column(row):
            return jnp.sum(jnp.where(spot, row, 0.0), axis=1, keepdims=True)

        attended = []
        for h in range(local_heads):
            row = slice(h, h + 1)
            acc = column(fresh[row] / total[row]) * placed_value[low : low + count]
            for t in range(n_tensor):
                piece = stat_in[t, first:last, :, h * width : (h + 1) * width].astype(f32)
                acc = acc + column(keeps[t][row] / total[row]) * piece.reshape(count, width)
            attended.append(acc)
        attended = jnp.concatenate(attended, axis=1).astype(bf16)
        part_out[low : low + count, :] = dot(attended, wo[...]).astype(bf16)
        to_sibling(part).start()

    def add(part):
        low, count = rows_of(part)
        to_sibling(part).wait()
        at = slice(low, low + count)
        pair = part_out[at, :].astype(f32) + part_in[at, :].astype(f32)
        sums[2 * low : 2 * low + count, :] = pair.astype(bf16)
        to_opposite(part).start()

    merge(0)
    add(0)
    merge(1)
    add(1)
    lanes = iota((rows, 2 * slots), 1)
    early = rows_of(0)[1]
    owner = jnp.where(
        lanes < 2 * early,
        lax.rem(lanes, early),
        early + lax.rem(lanes - 2 * early, slots - early),
    )
    back = (owner.astype(f32) == place).astype(bf16)
    to_opposite(0).wait()
    to_opposite(1).wait()
    out_ref[...] = dot(back, sums[...]).astype(bf16)
    wait_for(meta_in.at[pl.ds(0, n_dp - 1)], send_sem.at[0])
    for _ in range(n_tensor - 1):
        wait_for(q_in.at[:, 0], send_sem.at[1])
        wait_for(stat_in.at[0], send_sem.at[2])
        wait_for(small_in.at[0], send_sem.at[3])
    wait_for(q_in.at[pl.ds(0, n_dp - 1), 0], send_sem.at[1])
    wait_for(stat_in.at[0, pl.ds(0, n_dp - 1)], send_sem.at[2])
    wait_for(small_in.at[0, pl.ds(0, n_dp - 1)], send_sem.at[3])


def local(tokens, norm_gain, w_query, w_keyval, w_out, kv_pool, page_table, positions, assignment):
    n_dp, n_tensor = lax.axis_size("dp"), lax.axis_size("tensor")
    rows, model = tokens.shape
    width = w_keyval.shape[1] // 2
    query_width = w_query.shape[1]
    local_heads = query_width // width
    heads = local_heads * n_tensor
    capacity = max(8, rows // n_dp)
    slots = n_dp * capacity
    whole = pl.BlockSpec(memory_space=pltpu.VMEM)
    far = pl.BlockSpec(memory_space=pltpu.HBM)
    out = pl.pallas_call(
        functools.partial(kernel, n_dp, n_tensor, capacity),
        out_shape=pltpu.VMEM((rows, model), bf16),
        in_specs=[far] * 9,
        out_specs=whole,
        scratch_shapes=[
            pltpu.VMEM(tokens.shape, bf16),
            pltpu.VMEM((model // 128, 128), f32),
            pltpu.SMEM(page_table.shape[::-1], jnp.int32),
            pltpu.VMEM((1, rows), jnp.int32),
            pltpu.VMEM((1, rows), jnp.int32),
            pltpu.VMEM(w_query.shape, bf16),
            pltpu.VMEM(w_keyval.shape, bf16),
            pltpu.VMEM(w_out.shape, bf16),
            pltpu.VMEM(kv_pool.shape, bf16),
            pltpu.VMEM((n_dp, capacity, query_width), bf16),
            pltpu.VMEM((n_dp, 1, 128), jnp.int32),
            pltpu.VMEM((n_dp, n_tensor, capacity, query_width), bf16),
            pltpu.VMEM((n_dp, 1, 128), jnp.int32),
            pltpu.SMEM((n_dp, 1, 128), jnp.int32),
            pltpu.VMEM((capacity * heads, width), f32),
            pltpu.VMEM((capacity * heads, width), f32),
            pltpu.VMEM((n_dp, n_tensor, capacity, query_width), bf16),
            pltpu.VMEM((n_tensor, n_dp, capacity, query_width), bf16),
            pltpu.VMEM((n_dp, n_tensor, local_heads, 2 * slots), f32),
            pltpu.VMEM((n_tensor, n_dp, local_heads, 2 * slots), f32),
            pltpu.VMEM((slots, model), bf16),
            pltpu.VMEM((slots, model), bf16),
            pltpu.VMEM((2 * slots, model), bf16),
            pltpu.SemaphoreType.DMA((8,)),
            pltpu.SemaphoreType.DMA((chunks,)),
            pltpu.SemaphoreType.DMA((4,)),
            pltpu.SemaphoreType.DMA((8,)),
            pltpu.SemaphoreType.DMA((n_dp,)),
            pltpu.SemaphoreType.DMA((n_dp,)),
            pltpu.SemaphoreType.DMA((n_dp,)),
            pltpu.SemaphoreType.DMA((n_dp,)),
            pltpu.SemaphoreType.DMA((n_dp,)),
        ],
        compiler_params=pltpu.CompilerParams(
            collective_id=0, has_side_effects=True, vmem_limit_bytes=56 << 20
        ),
    )(
        tokens,
        norm_gain.reshape(model // 128, 128),
        w_query,
        w_keyval,
        w_out,
        kv_pool,
        page_table.T,
        positions.reshape(1, rows),
        assignment.reshape(1, rows),
    )
    return out


def solution(mesh):
    return jax.shard_map(
        local,
        mesh=mesh,
        in_specs=(
            P("dp", None),
            P(),
            P(None, "tensor"),
            P(),
            P("tensor", None),
            P(("dp", "tensor"), None, None),
            P("dp", "tensor"),
            P("dp"),
            P("dp"),
        ),
        out_specs=P("dp", None),
        check_vma=False,
    )
```

```python
import functools
import math

import jax
import jax.numpy as jnp
from jax import lax
from jax.experimental import pallas as pl
from jax.experimental.pallas import tpu as pltpu
from jax.sharding import PartitionSpec as P

masked_score = -1e30
peak_floor = -1e29
norm_eps = 1e-06
rotary_base = 10000.0
chunks = 8
MESH = pl.DeviceIdType.MESH
f32 = jnp.float32
bf16 = jnp.bfloat16


def dot(a, b):
    return jnp.dot(a, b, preferred_element_type=f32)


def dot_t(a, b):
    return lax.dot_general(a, b, (((1,), (1,)), ((), ())), preferred_element_type=f32)


def iota(shape, axis):
    return lax.broadcasted_iota(jnp.int32, shape, axis)


def xor(a, b, n):
    out, bit = 0, 1
    while bit < n:
        out = out + bit * lax.rem(lax.div(a, bit) + lax.div(b, bit), 2)
        bit *= 2
    return out


def order_of(n):
    return list(range(n//2))+list(range(n-1,n//2-1,-1))


def sends_of(n):
    return list(range(1,n))


def ends_of(n):
    return [n//2,n//2+n//4,n]


def pick(i, values):
    out = values[0]
    for k, value in enumerate(values[1:], 1):
        out = jnp.where(i == k, value, out)
    return out


def kernel(
    n_dp,
    n_tensor,
    capacity,
    tokens_hbm,
    gain_hbm,
    wq_hbm,
    wkv_hbm,
    wo_hbm,
    pool_hbm,
    table_hbm,
    position_hbm,
    assign_hbm,
    out_ref,
    tokens,
    gain_ref,
    table_ref,
    position_ref,
    assign_ref,
    wq,
    wkv,
    wo,
    pool,
    q_out,
    meta_out,
    q_in,
    meta_in,
    meta_s,
    group_q,
    group_acc,
    stat_out,
    stat_in,
    small_out,
    small_in,
    part_out,
    part_in,
    sums,
    load_sem,
    pool_sem,
    send_sem,
    sum_sem,
    meta_sem,
    smem_sem,
    q_sem,
    stat_sem,
    small_sem,
):
    dp = lax.axis_index("dp")
    tp = lax.axis_index("tensor")
    n_all = n_dp * n_tensor
    rows = tokens.shape[0]
    slots = n_dp * capacity
    width = wkv.shape[1] // 2
    half = width // 2
    local_heads = wq.shape[1] // width
    heads = local_heads * n_tensor
    pages, page_len = pool.shape[0], pool.shape[1]
    page_rows = table_ref.shape[0]
    window = page_rows * n_tensor * page_len
    chunk = pages // chunks
    scale = width ** (-0.5)
    order = order_of(n_dp)
    places = [order.index(k) for k in range(n_dp)]
    ends = ends_of(n_dp)
    spans = list(zip([0] + ends[:-1], ends))

    def partner(i):
        return xor(dp, pick(i, order), n_dp)

    barrier = pltpu.get_barrier_semaphore()

    loads = [
        pltpu.make_async_copy(src, dst, load_sem.at[i])
        for i, (src, dst) in enumerate(
            (
                (position_hbm, position_ref),
                (assign_hbm, assign_ref),
                (tokens_hbm, tokens),
                (gain_hbm, gain_ref),
                (wq_hbm, wq),
                (table_hbm, table_ref),
                (wkv_hbm, wkv),
                (wo_hbm, wo),
            )
        )
    ]
    for load in loads[:5]:
        load.start()

    @pl.loop(1, n_all)
    def _(i):
        k = n_all - i
        other = (xor(dp, lax.div(k, n_tensor), n_dp), xor(tp, lax.rem(k, n_tensor), n_tensor))
        pl.semaphore_signal(barrier, inc=1, device_id=other, device_id_type=MESH)

    def pool_load(i):
        part = pl.ds(i * chunk, chunk)
        return pltpu.make_async_copy(pool_hbm.at[part], pool.at[part], pool_sem.at[i])


    for load in loads[5:]:
        load.start()
    for i in range(chunks):
        pool_load(i).start()

    eye = iota((rows, rows), 0) == iota((rows, rows), 1)
    before = iota((rows, rows), 1) < iota((rows, rows), 0)
    after = iota((rows, rows), 1) > iota((rows, rows), 0)

    def as_column(row):
        return jnp.sum(jnp.where(eye, row, 0.0), axis=1, keepdims=True)

    loads[0].wait()
    loads[1].wait()
    position_row = position_ref[...].astype(f32)
    position = as_column(position_row)
    target_int = lax.div(assign_ref[...], rows)
    slot_row = (assign_ref[...] - target_int * rows).astype(f32)
    target_row = pick(target_int ^ dp, places).astype(f32)
    target = as_column(target_row)
    slot = as_column(slot_row)
    same = (target == target_row).astype(f32)
    place_row = target_row * capacity + jnp.sum(
        jnp.where(after, same, 0.0), axis=0, keepdims=True
    )
    within = jnp.sum(jnp.where(before, same, 0.0), axis=1, keepdims=True)
    place = target * capacity + within
    routed = (iota((slots, rows), 0).astype(f32) == place_row).astype(bf16)
    from_place = iota((rows, slots), 1).astype(f32) == place
    high = jnp.floor(position * (1.0 / 128.0))
    low = position - high * 128.0
    lane = iota((rows, 128), 1).astype(f32)
    fields = jnp.where(
        lane == within,
        slot,
        jnp.where(
            lane == within + capacity,
            high,
            jnp.where(lane == within + 2 * capacity, low, 0.0),
        ),
    ).astype(bf16)
    to_device = (iota((n_dp, rows), 0).astype(f32) == target_row).astype(bf16)
    meta = dot(to_device, fields).astype(jnp.int32)
    for d in range(n_dp):
        meta_out[d] = meta[d : d + 1, :]

    step = -2.0 * math.log(rotary_base) / width
    angles = position * jnp.exp(iota((1, half), 1).astype(f32) * step)
    cosine = jnp.cos(angles)
    sine = jnp.sin(angles)

    def rotate(values):
        first, second = values[:, :half], values[:, half:]
        return jnp.concatenate(
            [first * cosine - second * sine, first * sine + second * cosine], axis=1
        )

    loads[2].wait()
    loads[3].wait()
    gain = jnp.concatenate([gain_ref[i : i + 1, :] for i in range(gain_ref.shape[0])], axis=1)
    floats = tokens[...].astype(f32)
    normed = (
        floats
        * lax.rsqrt(jnp.mean(floats * floats, axis=-1, keepdims=True) + norm_eps)
        * gain
    ).astype(bf16)
    loads[4].wait()
    raw = dot(normed, wq[...])
    query = jnp.concatenate(
        [rotate(raw[:, h * width : (h + 1) * width]) for h in range(local_heads)], axis=1
    ).astype(bf16)
    q_out[...] = dot(routed, query).reshape(n_dp, capacity, local_heads * width).astype(bf16)

    pl.semaphore_wait(barrier, n_all - 1)

    def remote(src, dst, sent, received, where):
        return pltpu.make_async_remote_copy(
            src_ref=src,
            dst_ref=dst,
            send_sem=sent,
            recv_sem=received,
            device_id=where,
            device_id_type=MESH,
        )

    def wait_for(ref, sem):
        pltpu.make_async_copy(ref, ref, sem).wait()

    pltpu.make_async_copy(meta_out.at[0], meta_in.at[0], meta_sem.at[0]).start()

    @pl.loop(1, n_dp)
    def _(i):
        where = (partner(i), tp)
        remote(meta_out.at[i], meta_in.at[i], send_sem.at[0], meta_sem.at[i], where).start()

    pltpu.make_async_copy(q_out.at[0], q_in.at[0, tp], q_sem.at[0]).start()
    for k in range(1, n_tensor):
        where = (dp, xor(tp, k, n_tensor))
        remote(q_out.at[0], q_in.at[0, tp], send_sem.at[1], q_sem.at[0], where).start()

    @pl.loop(1, n_dp)
    def _(s):
        i = pick(s - 1, sends_of(n_dp))
        d = partner(i)
        for k in reversed(range(n_tensor)):
            where = (d, xor(tp, k, n_tensor))
            remote(q_out.at[i], q_in.at[i, tp], send_sem.at[1], q_sem.at[i], where).start()

    loads[6].wait()
    key_value = dot(normed, wkv[...])
    new_key = rotate(key_value[:, :width]).astype(bf16).astype(f32)
    new_value = key_value[:, width:].astype(bf16).astype(f32)
    own_scores = []
    for h in range(local_heads):
        product = query[:, h * width : (h + 1) * width].astype(f32) * new_key
        column = jnp.sum(product, axis=1, keepdims=True) * scale
        own_scores.append(jnp.sum(jnp.where(from_place, column, 0.0), axis=0, keepdims=True))
    own_score = jnp.concatenate(own_scores, axis=0)
    placed_value = dot(routed, new_value.astype(bf16))

    loads[5].wait()
    for i in range(chunks):
        pool_load(i).wait()

    lane_key = tp * page_rows * page_len + iota((heads, page_len), 1)
    stat_lane = iota((heads, 2 * slots), 1)

    def fetch(g):
        return pltpu.make_async_copy(meta_in.at[g], meta_s.at[g], smem_sem.at[g])

    def start_fetch(g):
        wait_for(meta_in.at[g], meta_sem.at[g])
        fetch(g).start()

    start_fetch(0)

    @pl.loop(0, n_dp)
    def _(g):
        d = partner(g)
        fetch(g).wait()

        @pl.when(g + 1 < n_dp)
        def _():
            start_fetch(g + 1)

        wait_for(q_in.at[g], q_sem.at[g])
        for t in range(n_tensor):
            part = q_in[g, t].astype(f32)
            for h in range(local_heads):
                group_q[pl.ds(t * local_heads + h, capacity, stride=heads), :] = part[
                    :, h * width : (h + 1) * width
                ]
        ids, scored = [], []
        for r in range(capacity):
            at = jnp.clip(meta_s[g, 0, r], 0, rows - 1)
            where = meta_s[g, 0, capacity + r] * 128 + meta_s[g, 0, 2 * capacity + r]
            ids.append([table_ref[j, at] for j in range(page_rows)])
            q = group_q[r * heads : (r + 1) * heads, :].astype(bf16)
            parts = []
            for j in range(page_rows):
                offset = (lane_key + (j * page_len) - where) & (window - 1)
                live = (offset != 0) & (offset >= window - where)
                keys = pool[ids[r][j], :, :width]
                parts.append(jnp.where(live, dot_t(q, keys) * scale, masked_score))
            scored.append(jnp.concatenate(parts, axis=1))
        packed = jnp.zeros((heads, 2 * slots), f32)
        for r in range(capacity):
            top = jnp.maximum(jnp.max(scored[r], axis=1, keepdims=True), peak_floor)
            weight = jnp.exp(scored[r] - top)
            total = jnp.sum(weight, axis=1, keepdims=True)
            values = jnp.concatenate(
                [pool[ids[r][j], :, width:] for j in range(page_rows)], axis=0
            )
            group_acc[r * heads : (r + 1) * heads, :] = dot(weight.astype(bf16), values)
            spot = g * capacity + r
            packed = jnp.where(stat_lane == spot, top, packed)
            packed = jnp.where(stat_lane == spot + slots, total, packed)
        for t in range(n_tensor):
            small_out[g, t] = packed[t * local_heads : (t + 1) * local_heads, :]
            stat_out[g, t] = jnp.concatenate(
                [
                    group_acc[pl.ds(t * local_heads + h, capacity, stride=heads), :]
                    for h in range(local_heads)
                ],
                axis=1,
            ).astype(bf16)

        for k in reversed(range(n_tensor)):
            t = xor(tp, k, n_tensor)
            pairs = (
                (small_out.at[g, t], small_in.at[tp, g], send_sem.at[3], small_sem.at[g]),
                (stat_out.at[g, t], stat_in.at[tp, g], send_sem.at[2], stat_sem.at[g]),
            )

            def send():
                for src, dst, sent, received in pairs:
                    remote(src, dst, sent, received, (d, t)).start()

            if k:
                send()
            else:
                pl.when(g > 0)(send)

                @pl.when(g == 0)
                def _():
                    for src, dst, sent, received in pairs:
                        pltpu.make_async_copy(src, dst, received).start()

    loads[7].wait()
    sibling = (dp, xor(tp, 1, n_tensor))
    opposite = (dp, xor(tp, 3, n_tensor))

    def rows_of(part):
        low, high = spans[part]
        return low * capacity, (high - low) * capacity

    def to_sibling(part):
        low, count = rows_of(part)
        at = pl.ds(low, count)
        return remote(
            part_out.at[at], part_in.at[at], sum_sem.at[part, 0], sum_sem.at[part, 1], sibling
        )

    def to_opposite(part):
        low, count = rows_of(part)
        own, other = pl.ds(2 * low, count), pl.ds(2 * low + count, count)
        return remote(
            sums.at[own], sums.at[other], sum_sem.at[part, 2], sum_sem.at[part, 3], opposite
        )

    def merge(part):
        first, last = spans[part]
        low, count = rows_of(part)

        @pl.loop(first, last)
        def _(g):
            wait_for(small_in.at[0, pl.ds(0, n_tensor)], small_sem.at[g])
            wait_for(stat_in.at[0, pl.ds(0, n_tensor)], stat_sem.at[g])

        tops, totals = [], []
        for t in range(n_tensor):
            merged = jnp.sum(small_in[t, first:last], axis=0)
            tops.append(merged[:, :slots])
            totals.append(merged[:, slots:])
        overall = functools.reduce(jnp.maximum, tops, own_score)
        fresh = jnp.exp(own_score - overall)
        keeps = [jnp.exp(top - overall) for top in tops]
        total = functools.reduce(jnp.add, [k * s for k, s in zip(keeps, totals)], fresh)
        spot = iota((count, slots), 1) == iota((count, slots), 0) + low

        def column(row):
            return jnp.sum(jnp.where(spot, row, 0.0), axis=1, keepdims=True)

        attended = []
        for h in range(local_heads):
            row = slice(h, h + 1)
            acc = column(fresh[row] / total[row]) * placed_value[low : low + count]
            for t in range(n_tensor):
                piece = stat_in[t, first:last, :, h * width : (h + 1) * width].astype(f32)
                acc = acc + column(keeps[t][row] / total[row]) * piece.reshape(count, width)
            attended.append(acc)
        attended = jnp.concatenate(attended, axis=1).astype(bf16)
        part_out[low : low + count, :] = dot(attended, wo[...]).astype(bf16)
        to_sibling(part).start()

    def add(part):
        low, count = rows_of(part)
        to_sibling(part).wait()
        at = slice(low, low + count)
        pair = part_out[at, :].astype(f32) + part_in[at, :].astype(f32)
        sums[2 * low : 2 * low + count, :] = pair.astype(bf16)
        to_opposite(part).start()

    lanes = iota((rows, 2 * slots), 1)
    owner = lanes
    for part in range(len(spans)):
        low, count = rows_of(part)
        owner = jnp.where(
            (lanes >= 2 * low) & (lanes < 2 * (low + count)),
            low + lax.rem(lanes - 2 * low, count),
            owner,
        )
    back = (owner.astype(f32) == place).astype(bf16)
    for part in range(len(spans)):
        merge(part)
        add(part)
    for part in range(len(spans)):
        to_opposite(part).wait()
    out_ref[...] = dot(back, sums[...]).astype(bf16)
    wait_for(meta_in.at[pl.ds(0, n_dp - 1)], send_sem.at[0])
    for _ in range(n_tensor - 1):
        wait_for(q_in.at[:, 0], send_sem.at[1])
        wait_for(stat_in.at[0], send_sem.at[2])
        wait_for(small_in.at[0], send_sem.at[3])
    wait_for(q_in.at[pl.ds(0, n_dp - 1), 0], send_sem.at[1])
    wait_for(stat_in.at[0, pl.ds(0, n_dp - 1)], send_sem.at[2])
    wait_for(small_in.at[0, pl.ds(0, n_dp - 1)], send_sem.at[3])


def local(tokens, norm_gain, w_query, w_keyval, w_out, kv_pool, page_table, positions, assignment):
    n_dp, n_tensor = lax.axis_size("dp"), lax.axis_size("tensor")
    rows, model = tokens.shape
    width = w_keyval.shape[1] // 2
    query_width = w_query.shape[1]
    local_heads = query_width // width
    heads = local_heads * n_tensor
    capacity = max(8, rows // n_dp)
    slots = n_dp * capacity
    whole = pl.BlockSpec(memory_space=pltpu.VMEM)
    far = pl.BlockSpec(memory_space=pltpu.HBM)
    out = pl.pallas_call(
        functools.partial(kernel, n_dp, n_tensor, capacity),
        out_shape=pltpu.VMEM((rows, model), bf16),
        in_specs=[far] * 9,
        out_specs=whole,
        scratch_shapes=[
            pltpu.VMEM(tokens.shape, bf16),
            pltpu.VMEM((model // 128, 128), f32),
            pltpu.SMEM(page_table.shape[::-1], jnp.int32),
            pltpu.VMEM((1, rows), jnp.int32),
            pltpu.VMEM((1, rows), jnp.int32),
            pltpu.VMEM(w_query.shape, bf16),
            pltpu.VMEM(w_keyval.shape, bf16),
            pltpu.VMEM(w_out.shape, bf16),
            pltpu.VMEM(kv_pool.shape, bf16),
            pltpu.VMEM((n_dp, capacity, query_width), bf16),
            pltpu.VMEM((n_dp, 1, 128), jnp.int32),
            pltpu.VMEM((n_dp, n_tensor, capacity, query_width), bf16),
            pltpu.VMEM((n_dp, 1, 128), jnp.int32),
            pltpu.SMEM((n_dp, 1, 128), jnp.int32),
            pltpu.VMEM((capacity * heads, width), f32),
            pltpu.VMEM((capacity * heads, width), f32),
            pltpu.VMEM((n_dp, n_tensor, capacity, query_width), bf16),
            pltpu.VMEM((n_tensor, n_dp, capacity, query_width), bf16),
            pltpu.VMEM((n_dp, n_tensor, local_heads, 2 * slots), f32),
            pltpu.VMEM((n_tensor, n_dp, local_heads, 2 * slots), f32),
            pltpu.VMEM((slots, model), bf16),
            pltpu.VMEM((slots, model), bf16),
            pltpu.VMEM((2 * slots, model), bf16),
            pltpu.SemaphoreType.DMA((8,)),
            pltpu.SemaphoreType.DMA((chunks,)),
            pltpu.SemaphoreType.DMA((4,)),
            pltpu.SemaphoreType.DMA((len(ends_of(n_dp)), 4)),
            pltpu.SemaphoreType.DMA((n_dp,)),
            pltpu.SemaphoreType.DMA((n_dp,)),
            pltpu.SemaphoreType.DMA((n_dp,)),
            pltpu.SemaphoreType.DMA((n_dp,)),
            pltpu.SemaphoreType.DMA((n_dp,)),
        ],
        compiler_params=pltpu.CompilerParams(
            collective_id=0, has_side_effects=True, vmem_limit_bytes=56 << 20
        ),
    )(
        tokens,
        norm_gain.reshape(model // 128, 128),
        w_query,
        w_keyval,
        w_out,
        kv_pool,
        page_table.T,
        positions.reshape(1, rows),
        assignment.reshape(1, rows),
    )
    return out


def solution(mesh):
    return jax.shard_map(
        local,
        mesh=mesh,
        in_specs=(
            P("dp", None),
            P(),
            P(None, "tensor"),
            P(),
            P("tensor", None),
            P(("dp", "tensor"), None, None),
            P("dp", "tensor"),
            P("dp"),
            P("dp"),
        ),
        out_specs=P("dp", None),
        check_vma=False,
    )
```

```python
import functools
import math

import jax
import jax.numpy as jnp
from jax import lax
from jax.experimental import pallas as pl
from jax.experimental.pallas import tpu as pltpu
from jax.sharding import PartitionSpec as P

masked_score = -1e30
peak_floor = -1e29
norm_eps = 1e-06
rotary_base = 10000.0
chunks = 8
MESH = pl.DeviceIdType.MESH
f32 = jnp.float32
bf16 = jnp.bfloat16


def dot(a, b):
    return jnp.dot(a, b, preferred_element_type=f32)


def dot_t(a, b):
    return lax.dot_general(a, b, (((1,), (1,)), ((), ())), preferred_element_type=f32)


def iota(shape, axis):
    return lax.broadcasted_iota(jnp.int32, shape, axis)


def xor(a, b, n):
    out, bit = 0, 1
    while bit < n:
        out = out + bit * lax.rem(lax.div(a, bit) + lax.div(b, bit), 2)
        bit *= 2
    return out


def ends_of(n):
    return [n // 2, n // 2 + n // 4, n]


def kernel(
    n_dp,
    n_tensor,
    capacity,
    tokens_hbm,
    gain_hbm,
    wq_hbm,
    wkv_hbm,
    wo_hbm,
    pool_hbm,
    table_hbm,
    position_hbm,
    assign_hbm,
    out_ref,
    tokens,
    gain_ref,
    table_ref,
    position_ref,
    assign_ref,
    wq,
    wkv,
    wo,
    pool,
    q_out,
    meta_out,
    q_in,
    meta_in,
    meta_s,
    group_q,
    group_acc,
    stat_out,
    stat_in,
    small_out,
    small_in,
    part_out,
    part_in,
    sums,
    load_sem,
    pool_sem,
    send_sem,
    sum_sem,
    meta_sem,
    smem_sem,
    q_sem,
    stat_sem,
    small_sem,
):
    dp = lax.axis_index("dp")
    tp = lax.axis_index("tensor")
    n_all = n_dp * n_tensor
    rows = tokens.shape[0]
    slots = n_dp * capacity
    width = wkv.shape[1] // 2
    half = width // 2
    local_heads = wq.shape[1] // width
    heads = local_heads * n_tensor
    pages, page_len = pool.shape[0], pool.shape[1]
    page_rows = table_ref.shape[0]
    window = page_rows * n_tensor * page_len
    chunk = pages // chunks
    scale = width ** (-0.5)
    ends = ends_of(n_dp)
    spans = list(zip([0] + ends[:-1], ends))

    def partner(i):
        return xor(dp, i, n_dp)

    barrier = pltpu.get_barrier_semaphore()

    loads = [
        pltpu.make_async_copy(src, dst, load_sem.at[i])
        for i, (src, dst) in enumerate(
            (
                (position_hbm, position_ref),
                (assign_hbm, assign_ref),
                (tokens_hbm, tokens),
                (gain_hbm, gain_ref),
                (wq_hbm, wq),
                (table_hbm, table_ref),
                (wkv_hbm, wkv),
                (wo_hbm, wo),
            )
        )
    ]
    for load in loads[:5]:
        load.start()

    @pl.loop(1, n_all)
    def _(i):
        k = n_all - i
        other = (xor(dp, lax.div(k, n_tensor), n_dp), xor(tp, lax.rem(k, n_tensor), n_tensor))
        pl.semaphore_signal(barrier, inc=1, device_id=other, device_id_type=MESH)

    def pool_load(i):
        part = pl.ds(i * chunk, chunk)
        return pltpu.make_async_copy(pool_hbm.at[part], pool.at[part], pool_sem.at[i])


    for load in loads[5:]:
        load.start()
    for i in range(chunks):
        pool_load(i).start()

    eye = iota((rows, rows), 0) == iota((rows, rows), 1)
    before = iota((rows, rows), 1) < iota((rows, rows), 0)
    after = iota((rows, rows), 1) > iota((rows, rows), 0)

    def as_column(row):
        return jnp.sum(jnp.where(eye, row, 0.0), axis=1, keepdims=True)

    loads[0].wait()
    loads[1].wait()
    position_row = position_ref[...].astype(f32)
    position = as_column(position_row)
    target_int = lax.div(assign_ref[...], rows)
    slot_row = (assign_ref[...] - target_int * rows).astype(f32)
    target_row = (target_int ^ dp).astype(f32)
    target = as_column(target_row)
    slot = as_column(slot_row)
    same = (target == target_row).astype(f32)
    place_row = target_row * capacity + jnp.sum(
        jnp.where(after, same, 0.0), axis=0, keepdims=True
    )
    within = jnp.sum(jnp.where(before, same, 0.0), axis=1, keepdims=True)
    place = target * capacity + within
    routed = (iota((slots, rows), 0).astype(f32) == place_row).astype(bf16)
    from_place = iota((rows, slots), 1).astype(f32) == place
    high = jnp.floor(position * (1.0 / 128.0))
    low = position - high * 128.0
    lane = iota((rows, 128), 1).astype(f32)
    fields = jnp.where(
        lane == within,
        slot,
        jnp.where(
            lane == within + capacity,
            high,
            jnp.where(lane == within + 2 * capacity, low, 0.0),
        ),
    ).astype(bf16)
    to_device = (iota((n_dp, rows), 0).astype(f32) == target_row).astype(bf16)
    meta = dot(to_device, fields).astype(jnp.int32)
    for d in range(n_dp):
        meta_out[d] = meta[d : d + 1, :]

    step = -2.0 * math.log(rotary_base) / width
    angles = position * jnp.exp(iota((1, half), 1).astype(f32) * step)
    cosine = jnp.cos(angles)
    sine = jnp.sin(angles)

    def rotate(values):
        first, second = values[:, :half], values[:, half:]
        return jnp.concatenate(
            [first * cosine - second * sine, first * sine + second * cosine], axis=1
        )

    loads[2].wait()
    loads[3].wait()
    gain = jnp.concatenate([gain_ref[i : i + 1, :] for i in range(gain_ref.shape[0])], axis=1)
    floats = tokens[...].astype(f32)
    normed = (
        floats
        * lax.rsqrt(jnp.mean(floats * floats, axis=-1, keepdims=True) + norm_eps)
        * gain
    ).astype(bf16)
    loads[4].wait()
    raw = dot(normed, wq[...])
    query = jnp.concatenate(
        [rotate(raw[:, h * width : (h + 1) * width]) for h in range(local_heads)], axis=1
    ).astype(bf16)
    q_out[...] = dot(routed, query).reshape(n_dp, capacity, local_heads * width).astype(bf16)

    pl.semaphore_wait(barrier, n_all - 1)

    def remote(src, dst, sent, received, where):
        return pltpu.make_async_remote_copy(
            src_ref=src,
            dst_ref=dst,
            send_sem=sent,
            recv_sem=received,
            device_id=where,
            device_id_type=MESH,
        )

    def wait_for(ref, sem):
        pltpu.make_async_copy(ref, ref, sem).wait()

    pltpu.make_async_copy(meta_out.at[0], meta_in.at[0], meta_sem.at[0]).start()

    @pl.loop(1, n_dp)
    def _(i):
        where = (partner(i), tp)
        remote(meta_out.at[i], meta_in.at[i], send_sem.at[0], meta_sem.at[i], where).start()

    pltpu.make_async_copy(q_out.at[0], q_in.at[0, tp], q_sem.at[0]).start()
    for k in range(1, n_tensor):
        where = (dp, xor(tp, k, n_tensor))
        remote(q_out.at[0], q_in.at[0, tp], send_sem.at[1], q_sem.at[0], where).start()

    @pl.loop(1, n_dp)
    def _(i):
        d = partner(i)
        for k in reversed(range(n_tensor)):
            where = (d, xor(tp, k, n_tensor))
            remote(q_out.at[i], q_in.at[i, tp], send_sem.at[1], q_sem.at[i], where).start()

    loads[6].wait()
    key_value = dot(normed, wkv[...])
    new_key = rotate(key_value[:, :width]).astype(bf16).astype(f32)
    new_value = key_value[:, width:].astype(bf16).astype(f32)
    own_scores = []
    for h in range(local_heads):
        product = query[:, h * width : (h + 1) * width].astype(f32) * new_key
        column = jnp.sum(product, axis=1, keepdims=True) * scale
        own_scores.append(jnp.sum(jnp.where(from_place, column, 0.0), axis=0, keepdims=True))
    own_score = jnp.concatenate(own_scores, axis=0)
    placed_value = dot(routed, new_value.astype(bf16))

    loads[5].wait()
    for i in range(chunks):
        pool_load(i).wait()

    lane_key = tp * page_rows * page_len + iota((heads, page_len), 1)
    stat_lane = iota((heads, 2 * slots), 1)

    def fetch(g):
        return pltpu.make_async_copy(meta_in.at[g], meta_s.at[g], smem_sem.at[g])

    def start_fetch(g):
        wait_for(meta_in.at[g], meta_sem.at[g])
        fetch(g).start()

    half_dp = n_dp // 2

    def group_of(i):
        home = i - half_dp + jnp.where(dp < half_dp, half_dp, 0)
        return jnp.where(i < half_dp, i, xor(dp, home, n_dp))

    start_fetch(group_of(0))

    @pl.loop(0, n_dp)
    def _(i):
        g = group_of(i)
        d = partner(g)
        fetch(g).wait()

        @pl.when(i + 1 < n_dp)
        def _():
            start_fetch(group_of(i + 1))

        wait_for(q_in.at[g], q_sem.at[g])
        for t in range(n_tensor):
            part = q_in[g, t].astype(f32)
            for h in range(local_heads):
                group_q[pl.ds(t * local_heads + h, capacity, stride=heads), :] = part[
                    :, h * width : (h + 1) * width
                ]
        ids, scored = [], []
        for r in range(capacity):
            at = jnp.clip(meta_s[g, 0, r], 0, rows - 1)
            where = meta_s[g, 0, capacity + r] * 128 + meta_s[g, 0, 2 * capacity + r]
            ids.append([table_ref[j, at] for j in range(page_rows)])
            q = group_q[r * heads : (r + 1) * heads, :].astype(bf16)
            parts = []
            for j in range(page_rows):
                offset = (lane_key + (j * page_len) - where) & (window - 1)
                live = (offset != 0) & (offset >= window - where)
                keys = pool[ids[r][j], :, :width]
                parts.append(jnp.where(live, dot_t(q, keys) * scale, masked_score))
            scored.append(jnp.concatenate(parts, axis=1))
        packed = jnp.zeros((heads, 2 * slots), f32)
        for r in range(capacity):
            top = jnp.maximum(jnp.max(scored[r], axis=1, keepdims=True), peak_floor)
            weight = jnp.exp(scored[r] - top)
            total = jnp.sum(weight, axis=1, keepdims=True)
            values = jnp.concatenate(
                [pool[ids[r][j], :, width:] for j in range(page_rows)], axis=0
            )
            group_acc[r * heads : (r + 1) * heads, :] = dot(weight.astype(bf16), values)
            spot = g * capacity + r
            packed = jnp.where(stat_lane == spot, top, packed)
            packed = jnp.where(stat_lane == spot + slots, total, packed)
        for t in range(n_tensor):
            small_out[g, t] = packed[t * local_heads : (t + 1) * local_heads, :]
            stat_out[g, t] = jnp.concatenate(
                [
                    group_acc[pl.ds(t * local_heads + h, capacity, stride=heads), :]
                    for h in range(local_heads)
                ],
                axis=1,
            ).astype(bf16)

        for k in reversed(range(n_tensor)):
            t = xor(tp, k, n_tensor)
            pairs = (
                (small_out.at[g, t], small_in.at[tp, g], send_sem.at[3], small_sem.at[g]),
                (stat_out.at[g, t], stat_in.at[tp, g], send_sem.at[2], stat_sem.at[g]),
            )

            def send():
                for src, dst, sent, received in pairs:
                    remote(src, dst, sent, received, (d, t)).start()

            if k:
                send()
            else:
                pl.when(g > 0)(send)

                @pl.when(g == 0)
                def _():
                    for src, dst, sent, received in pairs:
                        pltpu.make_async_copy(src, dst, received).start()

    loads[7].wait()
    sibling = (dp, xor(tp, 1, n_tensor))
    opposite = (dp, xor(tp, 3, n_tensor))

    def rows_of(part):
        low, high = spans[part]
        return low * capacity, (high - low) * capacity

    last_part = len(spans) - 1
    model_half = sums.shape[1] // 2
    core = lax.rem(tp, 2)

    def columns_of(part, other):
        if part == last_part:
            return pl.ds(0, 2 * model_half)
        side = 1 - core if other else core
        return pl.ds(pl.multiple_of(side * model_half, 128), model_half)

    def to_sibling(part):
        low, count = rows_of(part)
        at = pl.ds(low, count)
        return remote(
            part_out.at[at], part_in.at[at], sum_sem.at[part, 0], sum_sem.at[part, 1], sibling
        )

    def to_opposite(part):
        low, count = rows_of(part)
        own, other = pl.ds(2 * low, count), pl.ds(2 * low + count, count)
        return remote(
            sums.at[own, columns_of(part, 0)],
            sums.at[other, columns_of(part, 0)],
            sum_sem.at[part, 2],
            sum_sem.at[part, 3],
            opposite,
        )

    def pass_on(part):
        low, count = rows_of(part)
        got = sums.at[pl.ds(2 * low + count, count), columns_of(part, 1)]
        return remote(got, got, sum_sem.at[part, 4], sum_sem.at[part, 5], sibling)

    def merge(part):
        first, last = spans[part]
        low, count = rows_of(part)

        @pl.loop(first, last)
        def _(g):
            wait_for(small_in.at[0, pl.ds(0, n_tensor)], small_sem.at[g])
            wait_for(stat_in.at[0, pl.ds(0, n_tensor)], stat_sem.at[g])

        tops, totals = [], []
        for t in range(n_tensor):
            merged = jnp.sum(small_in[t, first:last], axis=0)
            tops.append(merged[:, :slots])
            totals.append(merged[:, slots:])
        overall = functools.reduce(jnp.maximum, tops, own_score)
        fresh = jnp.exp(own_score - overall)
        keeps = [jnp.exp(top - overall) for top in tops]
        total = functools.reduce(jnp.add, [k * s for k, s in zip(keeps, totals)], fresh)
        spot = iota((count, slots), 1) == iota((count, slots), 0) + low

        def column(row):
            return jnp.sum(jnp.where(spot, row, 0.0), axis=1, keepdims=True)

        attended = []
        for h in range(local_heads):
            row = slice(h, h + 1)
            acc = column(fresh[row] / total[row]) * placed_value[low : low + count]
            for t in range(n_tensor):
                piece = stat_in[t, first:last, :, h * width : (h + 1) * width].astype(f32)
                acc = acc + column(keeps[t][row] / total[row]) * piece.reshape(count, width)
            attended.append(acc)
        attended = jnp.concatenate(attended, axis=1).astype(bf16)
        part_out[low : low + count, :] = dot(attended, wo[...]).astype(bf16)
        to_sibling(part).start()

    def add(part):
        low, count = rows_of(part)
        to_sibling(part).wait()
        at = slice(low, low + count)
        pair = part_out[at, :].astype(f32) + part_in[at, :].astype(f32)
        sums[2 * low : 2 * low + count, :] = pair.astype(bf16)
        to_opposite(part).start()

    lanes = iota((rows, 2 * slots), 1)
    owner = lanes
    for part in range(len(spans)):
        low, count = rows_of(part)
        owner = jnp.where(
            (lanes >= 2 * low) & (lanes < 2 * (low + count)),
            low + lax.rem(lanes - 2 * low, count),
            owner,
        )
    back = (owner.astype(f32) == place).astype(bf16)
    merge(0)
    add(0)
    merge(1)
    merge(2)
    add(1)
    add(2)
    for part in range(last_part):
        to_opposite(part).wait()
        pass_on(part).start()
    to_opposite(last_part).wait()
    for part in range(last_part):
        pass_on(part).wait()
    out_ref[...] = dot(back, sums[...]).astype(bf16)
    wait_for(meta_in.at[pl.ds(0, n_dp - 1)], send_sem.at[0])
    for _ in range(n_tensor - 1):
        wait_for(q_in.at[:, 0], send_sem.at[1])
        wait_for(stat_in.at[0], send_sem.at[2])
        wait_for(small_in.at[0], send_sem.at[3])
    wait_for(q_in.at[pl.ds(0, n_dp - 1), 0], send_sem.at[1])
    wait_for(stat_in.at[0, pl.ds(0, n_dp - 1)], send_sem.at[2])
    wait_for(small_in.at[0, pl.ds(0, n_dp - 1)], send_sem.at[3])


def local(tokens, norm_gain, w_query, w_keyval, w_out, kv_pool, page_table, positions, assignment):
    n_dp, n_tensor = lax.axis_size("dp"), lax.axis_size("tensor")
    rows, model = tokens.shape
    width = w_keyval.shape[1] // 2
    query_width = w_query.shape[1]
    local_heads = query_width // width
    heads = local_heads * n_tensor
    capacity = max(8, rows // n_dp)
    slots = n_dp * capacity
    whole = pl.BlockSpec(memory_space=pltpu.VMEM)
    far = pl.BlockSpec(memory_space=pltpu.HBM)
    out = pl.pallas_call(
        functools.partial(kernel, n_dp, n_tensor, capacity),
        out_shape=pltpu.VMEM((rows, model), bf16),
        in_specs=[far] * 9,
        out_specs=whole,
        scratch_shapes=[
            pltpu.VMEM(tokens.shape, bf16),
            pltpu.VMEM((model // 128, 128), f32),
            pltpu.SMEM(page_table.shape[::-1], jnp.int32),
            pltpu.VMEM((1, rows), jnp.int32),
            pltpu.VMEM((1, rows), jnp.int32),
            pltpu.VMEM(w_query.shape, bf16),
            pltpu.VMEM(w_keyval.shape, bf16),
            pltpu.VMEM(w_out.shape, bf16),
            pltpu.VMEM(kv_pool.shape, bf16),
            pltpu.VMEM((n_dp, capacity, query_width), bf16),
            pltpu.VMEM((n_dp, 1, 128), jnp.int32),
            pltpu.VMEM((n_dp, n_tensor, capacity, query_width), bf16),
            pltpu.VMEM((n_dp, 1, 128), jnp.int32),
            pltpu.SMEM((n_dp, 1, 128), jnp.int32),
            pltpu.VMEM((capacity * heads, width), f32),
            pltpu.VMEM((capacity * heads, width), f32),
            pltpu.VMEM((n_dp, n_tensor, capacity, query_width), bf16),
            pltpu.VMEM((n_tensor, n_dp, capacity, query_width), bf16),
            pltpu.VMEM((n_dp, n_tensor, local_heads, 2 * slots), f32),
            pltpu.VMEM((n_tensor, n_dp, local_heads, 2 * slots), f32),
            pltpu.VMEM((slots, model), bf16),
            pltpu.VMEM((slots, model), bf16),
            pltpu.VMEM((2 * slots, model), bf16),
            pltpu.SemaphoreType.DMA((8,)),
            pltpu.SemaphoreType.DMA((chunks,)),
            pltpu.SemaphoreType.DMA((4,)),
            pltpu.SemaphoreType.DMA((len(ends_of(n_dp)), 6)),
            pltpu.SemaphoreType.DMA((n_dp,)),
            pltpu.SemaphoreType.DMA((n_dp,)),
            pltpu.SemaphoreType.DMA((n_dp,)),
            pltpu.SemaphoreType.DMA((n_dp,)),
            pltpu.SemaphoreType.DMA((n_dp,)),
        ],
        compiler_params=pltpu.CompilerParams(
            collective_id=0, has_side_effects=True, vmem_limit_bytes=56 << 20
        ),
    )(
        tokens,
        norm_gain.reshape(model // 128, 128),
        w_query,
        w_keyval,
        w_out,
        kv_pool,
        page_table.T,
        positions.reshape(1, rows),
        assignment.reshape(1, rows),
    )
    return out


def solution(mesh):
    return jax.shard_map(
        local,
        mesh=mesh,
        in_specs=(
            P("dp", None),
            P(),
            P(None, "tensor"),
            P(),
            P("tensor", None),
            P(("dp", "tensor"), None, None),
            P("dp", "tensor"),
            P("dp"),
            P("dp"),
        ),
        out_specs=P("dp", None),
        check_vma=False,
    )
```

```python
import functools
import math

import jax
import jax.numpy as jnp
from jax import lax
from jax.experimental import pallas as pl
from jax.experimental.pallas import tpu as pltpu
from jax.sharding import PartitionSpec as P

masked_score = -1e30
peak_floor = -1e29
norm_eps = 1e-06
rotary_base = 10000.0
chunks = 8
MESH = pl.DeviceIdType.MESH
f32 = jnp.float32
bf16 = jnp.bfloat16


def dot(a, b):
    return jnp.dot(a, b, preferred_element_type=f32)


def dot_t(a, b):
    return lax.dot_general(a, b, (((1,), (1,)), ((), ())), preferred_element_type=f32)


def iota(shape, axis):
    return lax.broadcasted_iota(jnp.int32, shape, axis)


def xor(a, b, n):
    out, bit = 0, 1
    while bit < n:
        out = out + bit * lax.rem(lax.div(a, bit) + lax.div(b, bit), 2)
        bit *= 2
    return out


def ends_of(n):
    return [n // 2, n // 2 + n // 4, n]


def kernel(
    n_dp,
    n_tensor,
    capacity,
    tokens_hbm,
    gain_hbm,
    wq_hbm,
    wkv_hbm,
    wo_hbm,
    pool_hbm,
    table_hbm,
    position_hbm,
    assign_hbm,
    out_ref,
    tokens,
    gain_ref,
    table_ref,
    position_ref,
    assign_ref,
    wq,
    wkv,
    wo,
    pool,
    q_out,
    meta_out,
    q_in,
    meta_in,
    meta_s,
    group_q,
    group_acc,
    stat_out,
    stat_in,
    small_out,
    small_in,
    part_out,
    part_in,
    sums,
    load_sem,
    pool_sem,
    send_sem,
    sum_sem,
    meta_sem,
    smem_sem,
    q_sem,
    stat_sem,
    small_sem,
):
    dp = lax.axis_index("dp")
    tp = lax.axis_index("tensor")
    n_all = n_dp * n_tensor
    rows = tokens.shape[0]
    slots = n_dp * capacity
    width = wkv.shape[1] // 2
    half = width // 2
    local_heads = wq.shape[1] // width
    heads = local_heads * n_tensor
    pages, page_len = pool.shape[0], pool.shape[1]
    page_rows = table_ref.shape[0]
    window = page_rows * n_tensor * page_len
    chunk = pages // chunks
    scale = width ** (-0.5)
    ends = ends_of(n_dp)
    spans = list(zip([0] + ends[:-1], ends))

    def partner(i):
        return xor(dp, i, n_dp)

    barrier = pltpu.get_barrier_semaphore()

    loads = [
        pltpu.make_async_copy(src, dst, load_sem.at[i])
        for i, (src, dst) in enumerate(
            (
                (position_hbm, position_ref),
                (assign_hbm, assign_ref),
                (tokens_hbm, tokens),
                (gain_hbm, gain_ref),
                (wq_hbm, wq),
                (table_hbm, table_ref),
                (wkv_hbm, wkv),
                (wo_hbm, wo),
            )
        )
    ]
    for load in loads[:5]:
        load.start()

    @pl.loop(1, n_all)
    def _(i):
        k = n_all - i
        other = (xor(dp, lax.div(k, n_tensor), n_dp), xor(tp, lax.rem(k, n_tensor), n_tensor))
        pl.semaphore_signal(barrier, inc=1, device_id=other, device_id_type=MESH)

    def pool_load(i):
        part = pl.ds(i * chunk, chunk)
        return pltpu.make_async_copy(pool_hbm.at[part], pool.at[part], pool_sem.at[i])


    for load in loads[5:]:
        load.start()
    for i in range(chunks):
        pool_load(i).start()

    eye = iota((rows, rows), 0) == iota((rows, rows), 1)
    before = iota((rows, rows), 1) < iota((rows, rows), 0)
    after = iota((rows, rows), 1) > iota((rows, rows), 0)

    def as_column(row):
        return jnp.sum(jnp.where(eye, row, 0.0), axis=1, keepdims=True)

    loads[0].wait()
    loads[1].wait()
    position_row = position_ref[...].astype(f32)
    position = as_column(position_row)
    target_int = lax.div(assign_ref[...], rows)
    slot_row = (assign_ref[...] - target_int * rows).astype(f32)
    target_row = (target_int ^ dp).astype(f32)
    target = as_column(target_row)
    slot = as_column(slot_row)
    same = (target == target_row).astype(f32)
    place_row = target_row * capacity + jnp.sum(
        jnp.where(after, same, 0.0), axis=0, keepdims=True
    )
    within = jnp.sum(jnp.where(before, same, 0.0), axis=1, keepdims=True)
    place = target * capacity + within
    routed = (iota((slots, rows), 0).astype(f32) == place_row).astype(bf16)
    from_place = iota((rows, slots), 1).astype(f32) == place
    high = jnp.floor(position * (1.0 / 128.0))
    low = position - high * 128.0
    lane = iota((rows, 128), 1).astype(f32)
    fields = jnp.where(
        lane == within,
        slot,
        jnp.where(
            lane == within + capacity,
            high,
            jnp.where(lane == within + 2 * capacity, low, 0.0),
        ),
    ).astype(bf16)
    to_device = (iota((n_dp, rows), 0).astype(f32) == target_row).astype(bf16)
    meta = dot(to_device, fields).astype(jnp.int32)
    for d in range(n_dp):
        meta_out[d] = meta[d : d + 1, :]

    step = -2.0 * math.log(rotary_base) / width
    angles = position * jnp.exp(iota((1, half), 1).astype(f32) * step)
    cosine = jnp.cos(angles)
    sine = jnp.sin(angles)

    def rotate(values):
        first, second = values[:, :half], values[:, half:]
        return jnp.concatenate(
            [first * cosine - second * sine, first * sine + second * cosine], axis=1
        )

    loads[2].wait()
    loads[3].wait()
    gain = jnp.concatenate([gain_ref[i : i + 1, :] for i in range(gain_ref.shape[0])], axis=1)
    floats = tokens[...].astype(f32)
    normed = (
        floats
        * lax.rsqrt(jnp.mean(floats * floats, axis=-1, keepdims=True) + norm_eps)
        * gain
    ).astype(bf16)
    loads[4].wait()
    raw = dot(normed, wq[...])
    query = jnp.concatenate(
        [rotate(raw[:, h * width : (h + 1) * width]) for h in range(local_heads)], axis=1
    ).astype(bf16)
    q_out[...] = dot(routed, query).reshape(n_dp, capacity, local_heads * width).astype(bf16)

    pl.semaphore_wait(barrier, n_all - 1)

    def remote(src, dst, sent, received, where):
        return pltpu.make_async_remote_copy(
            src_ref=src,
            dst_ref=dst,
            send_sem=sent,
            recv_sem=received,
            device_id=where,
            device_id_type=MESH,
        )

    def wait_for(ref, sem):
        pltpu.make_async_copy(ref, ref, sem).wait()

    pltpu.make_async_copy(meta_out.at[0], meta_in.at[0], meta_sem.at[0]).start()

    @pl.loop(1, n_dp)
    def _(i):
        where = (partner(i), tp)
        remote(meta_out.at[i], meta_in.at[i], send_sem.at[0], meta_sem.at[i], where).start()

    pltpu.make_async_copy(q_out.at[0], q_in.at[0, tp], q_sem.at[0]).start()
    for k in range(1, n_tensor):
        where = (dp, xor(tp, k, n_tensor))
        remote(q_out.at[0], q_in.at[0, tp], send_sem.at[1], q_sem.at[0], where).start()

    @pl.loop(1, n_dp)
    def _(i):
        d = partner(i)
        for k in reversed(range(n_tensor)):
            where = (d, xor(tp, k, n_tensor))
            remote(q_out.at[i], q_in.at[i, tp], send_sem.at[1], q_sem.at[i], where).start()

    loads[6].wait()
    key_value = dot(normed, wkv[...])
    new_key = rotate(key_value[:, :width]).astype(bf16).astype(f32)
    new_value = key_value[:, width:].astype(bf16).astype(f32)
    own_scores = []
    for h in range(local_heads):
        product = query[:, h * width : (h + 1) * width].astype(f32) * new_key
        column = jnp.sum(product, axis=1, keepdims=True) * scale
        own_scores.append(jnp.sum(jnp.where(from_place, column, 0.0), axis=0, keepdims=True))
    own_score = jnp.concatenate(own_scores, axis=0)
    placed_value = dot(routed, new_value.astype(bf16))

    loads[5].wait()
    for i in range(chunks):
        pool_load(i).wait()

    lane_key = tp * page_rows * page_len + iota((heads, page_rows * page_len), 1)
    stat_lane = iota((heads, 2 * slots), 1)

    def fetch(g):
        return pltpu.make_async_copy(meta_in.at[g], meta_s.at[g], smem_sem.at[g])

    def start_fetch(g):
        wait_for(meta_in.at[g], meta_sem.at[g])
        fetch(g).start()

    half_dp = n_dp // 2

    def group_of(i):
        home = i - half_dp + jnp.where(dp < half_dp, half_dp, 0)
        return jnp.where(i < half_dp, i, xor(dp, home, n_dp))

    start_fetch(group_of(0))

    @pl.loop(0, n_dp)
    def _(i):
        g = group_of(i)
        d = partner(g)
        fetch(g).wait()

        @pl.when(i + 1 < n_dp)
        def _():
            start_fetch(group_of(i + 1))

        wait_for(q_in.at[g], q_sem.at[g])
        for t in range(n_tensor):
            part = q_in[g, t].astype(f32)
            for h in range(local_heads):
                group_q[pl.ds(t * local_heads + h, capacity, stride=heads), :] = part[
                    :, h * width : (h + 1) * width
                ]
        ids, scored = [], []
        for r in range(capacity):
            at = jnp.clip(meta_s[g, 0, r], 0, rows - 1)
            where = meta_s[g, 0, capacity + r] * 128 + meta_s[g, 0, 2 * capacity + r]
            ids.append([table_ref[j, at] for j in range(page_rows)])
            q = group_q[r * heads : (r + 1) * heads, :].astype(bf16)
            keys = jnp.concatenate(
                [pool[ids[r][j], :, :width] for j in range(page_rows)], axis=0
            )
            offset = (lane_key - where) & (window - 1)
            live = (offset != 0) & (offset >= window - where)
            scored.append(jnp.where(live, dot_t(q, keys) * scale, masked_score))
        packed = jnp.zeros((heads, 2 * slots), f32)
        for r in range(capacity):
            top = jnp.maximum(jnp.max(scored[r], axis=1, keepdims=True), peak_floor)
            weight = jnp.exp(scored[r] - top)
            total = jnp.sum(weight, axis=1, keepdims=True)
            values = jnp.concatenate(
                [pool[ids[r][j], :, width:] for j in range(page_rows)], axis=0
            )
            group_acc[r * heads : (r + 1) * heads, :] = dot(weight.astype(bf16), values)
            spot = g * capacity + r
            packed = jnp.where(stat_lane == spot, top, packed)
            packed = jnp.where(stat_lane == spot + slots, total, packed)
        for t in range(n_tensor):
            small_out[g, t] = packed[t * local_heads : (t + 1) * local_heads, :]
            stat_out[g, t] = jnp.concatenate(
                [
                    group_acc[pl.ds(t * local_heads + h, capacity, stride=heads), :]
                    for h in range(local_heads)
                ],
                axis=1,
            ).astype(bf16)

        for k in reversed(range(n_tensor)):
            t = xor(tp, k, n_tensor)
            pairs = (
                (small_out.at[g, t], small_in.at[tp, g], send_sem.at[3], small_sem.at[g]),
                (stat_out.at[g, t], stat_in.at[tp, g], send_sem.at[2], stat_sem.at[g]),
            )

            def send():
                for src, dst, sent, received in pairs:
                    remote(src, dst, sent, received, (d, t)).start()

            if k:
                send()
            else:
                pl.when(g > 0)(send)

                @pl.when(g == 0)
                def _():
                    for src, dst, sent, received in pairs:
                        pltpu.make_async_copy(src, dst, received).start()

    loads[7].wait()
    sibling = (dp, xor(tp, 1, n_tensor))
    opposite = (dp, xor(tp, 3, n_tensor))

    def rows_of(part):
        low, high = spans[part]
        return low * capacity, (high - low) * capacity

    last_part = len(spans) - 1
    model_half = sums.shape[1] // 2
    core = lax.rem(tp, 2)

    def columns_of(part, other):
        if part == last_part:
            return pl.ds(0, 2 * model_half)
        side = 1 - core if other else core
        return pl.ds(pl.multiple_of(side * model_half, 128), model_half)

    def to_sibling(part):
        low, count = rows_of(part)
        at = pl.ds(low, count)
        return remote(
            part_out.at[at], part_in.at[at], sum_sem.at[part, 0], sum_sem.at[part, 1], sibling
        )

    def to_opposite(part):
        low, count = rows_of(part)
        own, other = pl.ds(2 * low, count), pl.ds(2 * low + count, count)
        return remote(
            sums.at[own, columns_of(part, 0)],
            sums.at[other, columns_of(part, 0)],
            sum_sem.at[part, 2],
            sum_sem.at[part, 3],
            opposite,
        )

    def pass_on(part):
        low, count = rows_of(part)
        got = sums.at[pl.ds(2 * low + count, count), columns_of(part, 1)]
        return remote(got, got, sum_sem.at[part, 4], sum_sem.at[part, 5], sibling)

    def merge(part):
        first, last = spans[part]
        low, count = rows_of(part)

        @pl.loop(first, last)
        def _(g):
            wait_for(small_in.at[0, pl.ds(0, n_tensor)], small_sem.at[g])
            wait_for(stat_in.at[0, pl.ds(0, n_tensor)], stat_sem.at[g])

        tops, totals = [], []
        for t in range(n_tensor):
            merged = jnp.sum(small_in[t, first:last], axis=0)
            tops.append(merged[:, :slots])
            totals.append(merged[:, slots:])
        overall = functools.reduce(jnp.maximum, tops, own_score)
        fresh = jnp.exp(own_score - overall)
        keeps = [jnp.exp(top - overall) for top in tops]
        total = functools.reduce(jnp.add, [k * s for k, s in zip(keeps, totals)], fresh)
        spot = iota((count, slots), 1) == iota((count, slots), 0) + low

        def column(row):
            return jnp.sum(jnp.where(spot, row, 0.0), axis=1, keepdims=True)

        attended = []
        for h in range(local_heads):
            row = slice(h, h + 1)
            acc = column(fresh[row] / total[row]) * placed_value[low : low + count]
            for t in range(n_tensor):
                piece = stat_in[t, first:last, :, h * width : (h + 1) * width].astype(f32)
                acc = acc + column(keeps[t][row] / total[row]) * piece.reshape(count, width)
            attended.append(acc)
        attended = jnp.concatenate(attended, axis=1).astype(bf16)
        part_out[low : low + count, :] = dot(attended, wo[...]).astype(bf16)
        to_sibling(part).start()

    def add(part):
        low, count = rows_of(part)
        to_sibling(part).wait()
        at = slice(low, low + count)
        pair = part_out[at, :].astype(f32) + part_in[at, :].astype(f32)
        sums[2 * low : 2 * low + count, :] = pair.astype(bf16)
        to_opposite(part).start()

    lanes = iota((rows, 2 * slots), 1)
    owner = lanes
    for part in range(len(spans)):
        low, count = rows_of(part)
        owner = jnp.where(
            (lanes >= 2 * low) & (lanes < 2 * (low + count)),
            low + lax.rem(lanes - 2 * low, count),
            owner,
        )
    back = (owner.astype(f32) == place).astype(bf16)
    merge(0)
    add(0)
    merge(1)
    merge(2)
    add(1)
    add(2)
    for part in range(last_part):
        to_opposite(part).wait()
        pass_on(part).start()
    to_opposite(last_part).wait()
    for part in range(last_part):
        pass_on(part).wait()
    out_ref[...] = dot(back, sums[...]).astype(bf16)
    wait_for(meta_in.at[pl.ds(0, n_dp - 1)], send_sem.at[0])
    for _ in range(n_tensor - 1):
        wait_for(q_in.at[:, 0], send_sem.at[1])
        wait_for(stat_in.at[0], send_sem.at[2])
        wait_for(small_in.at[0], send_sem.at[3])
    wait_for(q_in.at[pl.ds(0, n_dp - 1), 0], send_sem.at[1])
    wait_for(stat_in.at[0, pl.ds(0, n_dp - 1)], send_sem.at[2])
    wait_for(small_in.at[0, pl.ds(0, n_dp - 1)], send_sem.at[3])


def local(tokens, norm_gain, w_query, w_keyval, w_out, kv_pool, page_table, positions, assignment):
    n_dp, n_tensor = lax.axis_size("dp"), lax.axis_size("tensor")
    rows, model = tokens.shape
    width = w_keyval.shape[1] // 2
    query_width = w_query.shape[1]
    local_heads = query_width // width
    heads = local_heads * n_tensor
    capacity = max(8, rows // n_dp)
    slots = n_dp * capacity
    whole = pl.BlockSpec(memory_space=pltpu.VMEM)
    far = pl.BlockSpec(memory_space=pltpu.HBM)
    out = pl.pallas_call(
        functools.partial(kernel, n_dp, n_tensor, capacity),
        out_shape=pltpu.VMEM((rows, model), bf16),
        in_specs=[far] * 9,
        out_specs=whole,
        scratch_shapes=[
            pltpu.VMEM(tokens.shape, bf16),
            pltpu.VMEM((model // 128, 128), f32),
            pltpu.SMEM(page_table.shape[::-1], jnp.int32),
            pltpu.VMEM((1, rows), jnp.int32),
            pltpu.VMEM((1, rows), jnp.int32),
            pltpu.VMEM(w_query.shape, bf16),
            pltpu.VMEM(w_keyval.shape, bf16),
            pltpu.VMEM(w_out.shape, bf16),
            pltpu.VMEM(kv_pool.shape, bf16),
            pltpu.VMEM((n_dp, capacity, query_width), bf16),
            pltpu.VMEM((n_dp, 1, 128), jnp.int32),
            pltpu.VMEM((n_dp, n_tensor, capacity, query_width), bf16),
            pltpu.VMEM((n_dp, 1, 128), jnp.int32),
            pltpu.SMEM((n_dp, 1, 128), jnp.int32),
            pltpu.VMEM((capacity * heads, width), f32),
            pltpu.VMEM((capacity * heads, width), f32),
            pltpu.VMEM((n_dp, n_tensor, capacity, query_width), bf16),
            pltpu.VMEM((n_tensor, n_dp, capacity, query_width), bf16),
            pltpu.VMEM((n_dp, n_tensor, local_heads, 2 * slots), f32),
            pltpu.VMEM((n_tensor, n_dp, local_heads, 2 * slots), f32),
            pltpu.VMEM((slots, model), bf16),
            pltpu.VMEM((slots, model), bf16),
            pltpu.VMEM((2 * slots, model), bf16),
            pltpu.SemaphoreType.DMA((8,)),
            pltpu.SemaphoreType.DMA((chunks,)),
            pltpu.SemaphoreType.DMA((4,)),
            pltpu.SemaphoreType.DMA((len(ends_of(n_dp)), 6)),
            pltpu.SemaphoreType.DMA((n_dp,)),
            pltpu.SemaphoreType.DMA((n_dp,)),
            pltpu.SemaphoreType.DMA((n_dp,)),
            pltpu.SemaphoreType.DMA((n_dp,)),
            pltpu.SemaphoreType.DMA((n_dp,)),
        ],
        compiler_params=pltpu.CompilerParams(
            collective_id=0, has_side_effects=True, vmem_limit_bytes=56 << 20
        ),
    )(
        tokens,
        norm_gain.reshape(model // 128, 128),
        w_query,
        w_keyval,
        w_out,
        kv_pool,
        page_table.T,
        positions.reshape(1, rows),
        assignment.reshape(1, rows),
    )
    return out


def solution(mesh):
    return jax.shard_map(
        local,
        mesh=mesh,
        in_specs=(
            P("dp", None),
            P(),
            P(None, "tensor"),
            P(),
            P("tensor", None),
            P(("dp", "tensor"), None, None),
            P("dp", "tensor"),
            P("dp"),
            P("dp"),
        ),
        out_specs=P("dp", None),
        check_vma=False,
    )
```

```python
import functools
import math

import jax
import jax.numpy as jnp
from jax import lax
from jax.experimental import pallas as pl
from jax.experimental.pallas import tpu as pltpu
from jax.sharding import PartitionSpec as P

masked_score = -1e30
peak_floor = -1e29
norm_eps = 1e-06
rotary_base = 10000.0
chunks = 8
MESH = pl.DeviceIdType.MESH
f32 = jnp.float32
bf16 = jnp.bfloat16


def dot(a, b):
    return jnp.dot(a, b, preferred_element_type=f32)


def dot_t(a, b):
    return lax.dot_general(a, b, (((1,), (1,)), ((), ())), preferred_element_type=f32)


def iota(shape, axis):
    return lax.broadcasted_iota(jnp.int32, shape, axis)


def xor(a, b, n):
    out, bit = 0, 1
    while bit < n:
        out = out + bit * lax.rem(lax.div(a, bit) + lax.div(b, bit), 2)
        bit *= 2
    return out


def ends_of(n):
    return [n // 2, n // 2 + n // 4, n]


def kernel(
    n_dp,
    n_tensor,
    capacity,
    tokens_hbm,
    gain_hbm,
    wq_hbm,
    wkv_hbm,
    wo_hbm,
    pool_hbm,
    table_hbm,
    position_hbm,
    assign_hbm,
    out_ref,
    tokens,
    gain_ref,
    table_ref,
    position_ref,
    assign_ref,
    wq,
    wkv,
    wo,
    pool,
    q_out,
    meta_out,
    q_in,
    meta_in,
    meta_s,
    group_q,
    group_acc,
    stat_out,
    stat_in,
    small_out,
    small_in,
    part_out,
    part_in,
    sums,
    load_sem,
    pool_sem,
    send_sem,
    sum_sem,
    meta_sem,
    smem_sem,
    q_sem,
    stat_sem,
    small_sem,
):
    dp = lax.axis_index("dp")
    tp = lax.axis_index("tensor")
    n_all = n_dp * n_tensor
    rows = tokens.shape[0]
    slots = n_dp * capacity
    width = wkv.shape[1] // 2
    half = width // 2
    local_heads = wq.shape[1] // width
    heads = local_heads * n_tensor
    pages, page_len = pool.shape[0], pool.shape[1]
    page_rows = table_ref.shape[0]
    window = page_rows * n_tensor * page_len
    chunk = pages // chunks
    scale = width ** (-0.5)
    ends = ends_of(n_dp)
    spans = list(zip([0] + ends[:-1], ends))

    def partner(i):
        return xor(dp, i, n_dp)

    barrier = pltpu.get_barrier_semaphore()

    loads = [
        pltpu.make_async_copy(src, dst, load_sem.at[i])
        for i, (src, dst) in enumerate(
            (
                (position_hbm, position_ref),
                (assign_hbm, assign_ref),
                (tokens_hbm, tokens),
                (gain_hbm, gain_ref),
                (wq_hbm, wq),
                (table_hbm, table_ref),
                (wkv_hbm, wkv),
                (wo_hbm, wo),
            )
        )
    ]
    for load in loads[:5]:
        load.start()

    @pl.loop(1, n_all)
    def _(i):
        k = n_all - i
        other = (xor(dp, lax.div(k, n_tensor), n_dp), xor(tp, lax.rem(k, n_tensor), n_tensor))
        pl.semaphore_signal(barrier, inc=1, device_id=other, device_id_type=MESH)

    def pool_load(i):
        part = pl.ds(i * chunk, chunk)
        return pltpu.make_async_copy(pool_hbm.at[part], pool.at[part], pool_sem.at[i])


    eye = iota((rows, rows), 0) == iota((rows, rows), 1)
    before = iota((rows, rows), 1) < iota((rows, rows), 0)
    after = iota((rows, rows), 1) > iota((rows, rows), 0)

    def as_column(row):
        return jnp.sum(jnp.where(eye, row, 0.0), axis=1, keepdims=True)

    loads[0].wait()
    loads[1].wait()
    position_row = position_ref[...].astype(f32)
    position = as_column(position_row)
    target_int = lax.div(assign_ref[...], rows)
    slot_row = (assign_ref[...] - target_int * rows).astype(f32)
    target_row = (target_int ^ dp).astype(f32)
    target = as_column(target_row)
    slot = as_column(slot_row)
    same = (target == target_row).astype(f32)
    place_row = target_row * capacity + jnp.sum(
        jnp.where(after, same, 0.0), axis=0, keepdims=True
    )
    within = jnp.sum(jnp.where(before, same, 0.0), axis=1, keepdims=True)
    place = target * capacity + within
    routed = (iota((slots, rows), 0).astype(f32) == place_row).astype(bf16)
    from_place = iota((rows, slots), 1).astype(f32) == place
    high = jnp.floor(position * (1.0 / 128.0))
    low = position - high * 128.0
    lane = iota((rows, 128), 1).astype(f32)
    fields = jnp.where(
        lane == within,
        slot,
        jnp.where(
            lane == within + capacity,
            high,
            jnp.where(lane == within + 2 * capacity, low, 0.0),
        ),
    ).astype(bf16)
    to_device = (iota((n_dp, rows), 0).astype(f32) == target_row).astype(bf16)
    meta = dot(to_device, fields).astype(jnp.int32)
    for d in range(n_dp):
        meta_out[d] = meta[d : d + 1, :]

    step = -2.0 * math.log(rotary_base) / width
    angles = position * jnp.exp(iota((1, half), 1).astype(f32) * step)
    cosine = jnp.cos(angles)
    sine = jnp.sin(angles)

    def rotate(values):
        first, second = values[:, :half], values[:, half:]
        return jnp.concatenate(
            [first * cosine - second * sine, first * sine + second * cosine], axis=1
        )

    loads[2].wait()
    loads[3].wait()
    gain = jnp.concatenate([gain_ref[i : i + 1, :] for i in range(gain_ref.shape[0])], axis=1)
    floats = tokens[...].astype(f32)
    normed = (
        floats
        * lax.rsqrt(jnp.mean(floats * floats, axis=-1, keepdims=True) + norm_eps)
        * gain
    ).astype(bf16)
    loads[4].wait()
    for load in loads[5:]:
        load.start()
    for i in range(chunks):
        pool_load(i).start()
    raw = dot(normed, wq[...])
    query = jnp.concatenate(
        [rotate(raw[:, h * width : (h + 1) * width]) for h in range(local_heads)], axis=1
    ).astype(bf16)
    q_out[...] = dot(routed, query).reshape(n_dp, capacity, local_heads * width).astype(bf16)

    pl.semaphore_wait(barrier, n_all - 1)

    def remote(src, dst, sent, received, where):
        return pltpu.make_async_remote_copy(
            src_ref=src,
            dst_ref=dst,
            send_sem=sent,
            recv_sem=received,
            device_id=where,
            device_id_type=MESH,
        )

    def wait_for(ref, sem):
        pltpu.make_async_copy(ref, ref, sem).wait()

    pltpu.make_async_copy(meta_out.at[0], meta_in.at[0], meta_sem.at[0]).start()

    @pl.loop(1, n_dp)
    def _(i):
        where = (partner(i), tp)
        remote(meta_out.at[i], meta_in.at[i], send_sem.at[0], meta_sem.at[i], where).start()

    pltpu.make_async_copy(q_out.at[0], q_in.at[0, tp], q_sem.at[0]).start()
    for k in range(1, n_tensor):
        where = (dp, xor(tp, k, n_tensor))
        remote(q_out.at[0], q_in.at[0, tp], send_sem.at[1], q_sem.at[0], where).start()

    @pl.loop(1, n_dp)
    def _(i):
        d = partner(i)
        for k in reversed(range(n_tensor)):
            where = (d, xor(tp, k, n_tensor))
            remote(q_out.at[i], q_in.at[i, tp], send_sem.at[1], q_sem.at[i], where).start()

    loads[6].wait()
    key_value = dot(normed, wkv[...])
    new_key = rotate(key_value[:, :width]).astype(bf16).astype(f32)
    new_value = key_value[:, width:].astype(bf16).astype(f32)
    own_scores = []
    for h in range(local_heads):
        product = query[:, h * width : (h + 1) * width].astype(f32) * new_key
        column = jnp.sum(product, axis=1, keepdims=True) * scale
        own_scores.append(jnp.sum(jnp.where(from_place, column, 0.0), axis=0, keepdims=True))
    own_score = jnp.concatenate(own_scores, axis=0)
    placed_value = dot(routed, new_value.astype(bf16))

    loads[5].wait()
    for i in range(chunks):
        pool_load(i).wait()

    lane_key = tp * page_rows * page_len + iota((heads, page_rows * page_len), 1)
    stat_lane = iota((heads, 2 * slots), 1)

    def fetch(g):
        return pltpu.make_async_copy(meta_in.at[g], meta_s.at[g], smem_sem.at[g])

    def start_fetch(g):
        wait_for(meta_in.at[g], meta_sem.at[g])
        fetch(g).start()

    half_dp = n_dp // 2

    def group_of(i):
        home = i - half_dp + jnp.where(dp < half_dp, half_dp, 0)
        return jnp.where(i < half_dp, i, xor(dp, home, n_dp))

    start_fetch(group_of(0))

    @pl.loop(0, n_dp)
    def _(i):
        g = group_of(i)
        d = partner(g)
        fetch(g).wait()

        @pl.when(i + 1 < n_dp)
        def _():
            start_fetch(group_of(i + 1))

        wait_for(q_in.at[g], q_sem.at[g])
        for t in range(n_tensor):
            part = q_in[g, t].astype(f32)
            for h in range(local_heads):
                group_q[pl.ds(t * local_heads + h, capacity, stride=heads), :] = part[
                    :, h * width : (h + 1) * width
                ]
        ids, scored = [], []
        for r in range(capacity):
            at = jnp.clip(meta_s[g, 0, r], 0, rows - 1)
            where = meta_s[g, 0, capacity + r] * 128 + meta_s[g, 0, 2 * capacity + r]
            ids.append([table_ref[j, at] for j in range(page_rows)])
            q = group_q[r * heads : (r + 1) * heads, :].astype(bf16)
            keys = jnp.concatenate(
                [pool[ids[r][j], :, :width] for j in range(page_rows)], axis=0
            )
            offset = (lane_key - where) & (window - 1)
            live = (offset != 0) & (offset >= window - where)
            scored.append(jnp.where(live, dot_t(q, keys) * scale, masked_score))
        packed = jnp.zeros((heads, 2 * slots), f32)
        for r in range(capacity):
            top = jnp.maximum(jnp.max(scored[r], axis=1, keepdims=True), peak_floor)
            weight = jnp.exp(scored[r] - top)
            total = jnp.sum(weight, axis=1, keepdims=True)
            values = jnp.concatenate(
                [pool[ids[r][j], :, width:] for j in range(page_rows)], axis=0
            )
            group_acc[r * heads : (r + 1) * heads, :] = dot(weight.astype(bf16), values)
            spot = g * capacity + r
            packed = jnp.where(stat_lane == spot, top, packed)
            packed = jnp.where(stat_lane == spot + slots, total, packed)
        for t in range(n_tensor):
            small_out[g, t] = packed[t * local_heads : (t + 1) * local_heads, :]
            stat_out[g, t] = jnp.concatenate(
                [
                    group_acc[pl.ds(t * local_heads + h, capacity, stride=heads), :]
                    for h in range(local_heads)
                ],
                axis=1,
            ).astype(bf16)

        for k in reversed(range(n_tensor)):
            t = xor(tp, k, n_tensor)
            pairs = (
                (small_out.at[g, t], small_in.at[tp, g], send_sem.at[3], small_sem.at[g]),
                (stat_out.at[g, t], stat_in.at[tp, g], send_sem.at[2], stat_sem.at[g]),
            )

            def send():
                for src, dst, sent, received in pairs:
                    remote(src, dst, sent, received, (d, t)).start()

            if k:
                send()
            else:
                pl.when(g > 0)(send)

                @pl.when(g == 0)
                def _():
                    for src, dst, sent, received in pairs:
                        pltpu.make_async_copy(src, dst, received).start()

    loads[7].wait()
    sibling = (dp, xor(tp, 1, n_tensor))
    opposite = (dp, xor(tp, 3, n_tensor))

    def rows_of(part):
        low, high = spans[part]
        return low * capacity, (high - low) * capacity

    last_part = len(spans) - 1
    model_half = sums.shape[1] // 2
    core = lax.rem(tp, 2)

    def columns_of(part, other):
        if part == last_part:
            return pl.ds(0, 2 * model_half)
        side = 1 - core if other else core
        return pl.ds(pl.multiple_of(side * model_half, 128), model_half)

    def to_sibling(part):
        low, count = rows_of(part)
        at = pl.ds(low, count)
        return remote(
            part_out.at[at], part_in.at[at], sum_sem.at[part, 0], sum_sem.at[part, 1], sibling
        )

    def to_opposite(part):
        low, count = rows_of(part)
        own, other = pl.ds(2 * low, count), pl.ds(2 * low + count, count)
        return remote(
            sums.at[own, columns_of(part, 0)],
            sums.at[other, columns_of(part, 0)],
            sum_sem.at[part, 2],
            sum_sem.at[part, 3],
            opposite,
        )

    def pass_on(part):
        low, count = rows_of(part)
        got = sums.at[pl.ds(2 * low + count, count), columns_of(part, 1)]
        return remote(got, got, sum_sem.at[part, 4], sum_sem.at[part, 5], sibling)

    def merge(part):
        first, last = spans[part]
        low, count = rows_of(part)

        @pl.loop(first, last)
        def _(g):
            wait_for(small_in.at[0, pl.ds(0, n_tensor)], small_sem.at[g])
            wait_for(stat_in.at[0, pl.ds(0, n_tensor)], stat_sem.at[g])

        tops, totals = [], []
        for t in range(n_tensor):
            merged = jnp.sum(small_in[t, first:last], axis=0)
            tops.append(merged[:, :slots])
            totals.append(merged[:, slots:])
        overall = functools.reduce(jnp.maximum, tops, own_score)
        fresh = jnp.exp(own_score - overall)
        keeps = [jnp.exp(top - overall) for top in tops]
        total = functools.reduce(jnp.add, [k * s for k, s in zip(keeps, totals)], fresh)
        spot = iota((count, slots), 1) == iota((count, slots), 0) + low

        def column(row):
            return jnp.sum(jnp.where(spot, row, 0.0), axis=1, keepdims=True)

        attended = []
        for h in range(local_heads):
            row = slice(h, h + 1)
            acc = column(fresh[row] / total[row]) * placed_value[low : low + count]
            for t in range(n_tensor):
                piece = stat_in[t, first:last, :, h * width : (h + 1) * width].astype(f32)
                acc = acc + column(keeps[t][row] / total[row]) * piece.reshape(count, width)
            attended.append(acc)
        attended = jnp.concatenate(attended, axis=1).astype(bf16)
        part_out[low : low + count, :] = dot(attended, wo[...]).astype(bf16)
        to_sibling(part).start()

    def add(part):
        low, count = rows_of(part)
        to_sibling(part).wait()
        at = slice(low, low + count)
        pair = part_out[at, :].astype(f32) + part_in[at, :].astype(f32)
        sums[2 * low : 2 * low + count, :] = pair.astype(bf16)
        to_opposite(part).start()

    lanes = iota((rows, 2 * slots), 1)
    owner = lanes
    for part in range(len(spans)):
        low, count = rows_of(part)
        owner = jnp.where(
            (lanes >= 2 * low) & (lanes < 2 * (low + count)),
            low + lax.rem(lanes - 2 * low, count),
            owner,
        )
    back = (owner.astype(f32) == place).astype(bf16)
    merge(0)
    add(0)
    merge(1)
    merge(2)
    add(1)
    add(2)
    for part in range(last_part):
        to_opposite(part).wait()
        pass_on(part).start()
    to_opposite(last_part).wait()
    for part in range(last_part):
        pass_on(part).wait()
    out_ref[...] = dot(back, sums[...]).astype(bf16)
    wait_for(meta_in.at[pl.ds(0, n_dp - 1)], send_sem.at[0])
    for _ in range(n_tensor - 1):
        wait_for(q_in.at[:, 0], send_sem.at[1])
        wait_for(stat_in.at[0], send_sem.at[2])
        wait_for(small_in.at[0], send_sem.at[3])
    wait_for(q_in.at[pl.ds(0, n_dp - 1), 0], send_sem.at[1])
    wait_for(stat_in.at[0, pl.ds(0, n_dp - 1)], send_sem.at[2])
    wait_for(small_in.at[0, pl.ds(0, n_dp - 1)], send_sem.at[3])


def local(tokens, norm_gain, w_query, w_keyval, w_out, kv_pool, page_table, positions, assignment):
    n_dp, n_tensor = lax.axis_size("dp"), lax.axis_size("tensor")
    rows, model = tokens.shape
    width = w_keyval.shape[1] // 2
    query_width = w_query.shape[1]
    local_heads = query_width // width
    heads = local_heads * n_tensor
    capacity = max(8, rows // n_dp)
    slots = n_dp * capacity
    whole = pl.BlockSpec(memory_space=pltpu.VMEM)
    far = pl.BlockSpec(memory_space=pltpu.HBM)
    out = pl.pallas_call(
        functools.partial(kernel, n_dp, n_tensor, capacity),
        out_shape=pltpu.VMEM((rows, model), bf16),
        in_specs=[far] * 9,
        out_specs=whole,
        scratch_shapes=[
            pltpu.VMEM(tokens.shape, bf16),
            pltpu.VMEM((model // 128, 128), f32),
            pltpu.SMEM(page_table.shape[::-1], jnp.int32),
            pltpu.VMEM((1, rows), jnp.int32),
            pltpu.VMEM((1, rows), jnp.int32),
            pltpu.VMEM(w_query.shape, bf16),
            pltpu.VMEM(w_keyval.shape, bf16),
            pltpu.VMEM(w_out.shape, bf16),
            pltpu.VMEM(kv_pool.shape, bf16),
            pltpu.VMEM((n_dp, capacity, query_width), bf16),
            pltpu.VMEM((n_dp, 1, 128), jnp.int32),
            pltpu.VMEM((n_dp, n_tensor, capacity, query_width), bf16),
            pltpu.VMEM((n_dp, 1, 128), jnp.int32),
            pltpu.SMEM((n_dp, 1, 128), jnp.int32),
            pltpu.VMEM((capacity * heads, width), f32),
            pltpu.VMEM((capacity * heads, width), f32),
            pltpu.VMEM((n_dp, n_tensor, capacity, query_width), bf16),
            pltpu.VMEM((n_tensor, n_dp, capacity, query_width), bf16),
            pltpu.VMEM((n_dp, n_tensor, local_heads, 2 * slots), f32),
            pltpu.VMEM((n_tensor, n_dp, local_heads, 2 * slots), f32),
            pltpu.VMEM((slots, model), bf16),
            pltpu.VMEM((slots, model), bf16),
            pltpu.VMEM((2 * slots, model), bf16),
            pltpu.SemaphoreType.DMA((8,)),
            pltpu.SemaphoreType.DMA((chunks,)),
            pltpu.SemaphoreType.DMA((4,)),
            pltpu.SemaphoreType.DMA((len(ends_of(n_dp)), 6)),
            pltpu.SemaphoreType.DMA((n_dp,)),
            pltpu.SemaphoreType.DMA((n_dp,)),
            pltpu.SemaphoreType.DMA((n_dp,)),
            pltpu.SemaphoreType.DMA((n_dp,)),
            pltpu.SemaphoreType.DMA((n_dp,)),
        ],
        compiler_params=pltpu.CompilerParams(
            collective_id=0, has_side_effects=True, vmem_limit_bytes=56 << 20
        ),
    )(
        tokens,
        norm_gain.reshape(model // 128, 128),
        w_query,
        w_keyval,
        w_out,
        kv_pool,
        page_table.T,
        positions.reshape(1, rows),
        assignment.reshape(1, rows),
    )
    return out


def solution(mesh):
    return jax.shard_map(
        local,
        mesh=mesh,
        in_specs=(
            P("dp", None),
            P(),
            P(None, "tensor"),
            P(),
            P("tensor", None),
            P(("dp", "tensor"), None, None),
            P("dp", "tensor"),
            P("dp"),
            P("dp"),
        ),
        out_specs=P("dp", None),
        check_vma=False,
    )
```
